128 devices in a mesh: src: 16 (over y_hi, z, core), rep: 8 (over y_lo, x).
Axes of the slice: x: 4, y: 4 (y_hi: 2, y_lo: 2; y = y_hi * 2 + y_lo), z: 4, core: 2. Of those that a mesh axis runs over, the one named last changes fastest.
Arguments:
- queries: bfloat16 [16384, 512], P(('src', 'rep')), may hold values from -6 to 6
- out_grad: bfloat16 [16384, 512], P(('src', 'rep')), may hold values from -48 to 48
- outputs: bfloat16 [16384, 512], P(('src', 'rep')), may hold values from -6 to 6
- log_norms: float32 [4, 16384], P(None, ('src', 'rep')), may hold values from 6 to 8
- src_keys: bfloat16 [16384, 512], P('src'), may hold values from -6 to 6
- src_values: bfloat16 [16384, 512], P('src'), may hold values from -6 to 6
- block_list: int32 [16, 8, 2, 96], P('src', 'rep'), may hold values from 0 to 15, as said below
- block_count: int32 [16, 8], P('src', 'rep'), may hold values from 1 to 96, as said below
- mask_bits: int32 [16, 8, 96, 8, 128], P('src', 'rep'), may hold values from 0 to 65535
Outputs:
- query_grad: bfloat16 [16384, 512], P(('src', 'rep'))
- key_grad: bfloat16 [16384, 512], P(('src', 'rep'))
- value_grad: bfloat16 [16384, 512], P(('src', 'rep'))
The draws below stay inside these ranges and needn't reach their ends.
Inputs may be any that keep to these rules, and one draw needn't show every extreme that they name: `block_list`: row 0 holds destination blocks 0 to 15 of the group, row 1 source blocks 0 to 7 of the shard; the 96 pairs of one (s, r) are distinct. `block_count`: one source shard has 96 live entries in every group. `mask_bits`: bit b (counted from the lowest) of word w at column c is the edge from source row c to destination row 16 w + b of the block pair; bits for rows at or past 128, where there are any, are ignored.
All inputs are finite; a program needn't handle non-finite values.
Results may differ from the reference program's by a relative error of at most 0.0049.
Values may be sent and summed in bfloat16 or wider, within the bound.
A program may use at most 64 MiB of HBM per device.

```python
import jax
import jax.numpy as jnp
from jax import lax

HEADS = 4
HEAD_DIM = 128
BLOCK = 128
SRC_BLKS = 8
CAP = 96
NODES = 16384
DST_BLKS = 16
WORDS = 8
N_SRC = 16
N_REP = 8


def draw_block_list(key, part):
    device_keys = jax.random.split(jax.random.fold_in(key, 3), N_SRC * N_REP)
    pair_codes = jax.vmap(lambda single: jax.random.permutation(single, DST_BLKS * SRC_BLKS)[:CAP])(device_keys)
    pair_codes = pair_codes.astype(jnp.int32)
    stacked = jnp.stack([pair_codes // SRC_BLKS, pair_codes % SRC_BLKS], axis=1)
    return stacked.reshape(N_SRC, N_REP, 2, CAP).astype(jnp.int32)


def draw_block_count(key, part):
    heavy_shard = jax.random.randint(jax.random.fold_in(key, 5), (), 0, N_SRC, dtype=jnp.int32)
    load_level = jax.random.randint(jax.random.fold_in(key, 7), (N_SRC, N_REP), 1, 4, dtype=jnp.int32)
    light_count = jnp.maximum(1, CAP * load_level // 8)
    shard_ids = jnp.arange(N_SRC, dtype=jnp.int32)[:, None]
    return jnp.where(shard_ids == heavy_shard, CAP, light_count).astype(jnp.int32)


def place_ends(drawn, rng, low, top_value):
    dims = drawn.shape
    index_at = [jax.random.randint(jax.random.fold_in(rng, axis), (), 0, dims[axis]) for axis in range(len(dims))]
    drawn = drawn.at[tuple(index_at)].set(low)
    longest = dims.index(max(dims))
    index_at[longest] = (index_at[longest] + 1) % dims[longest]
    return drawn.at[tuple(index_at)].set(top_value)


def block_levels(stream_key, extent, shards, low, high):
    level = 1.0
    for axis_at, parts in shards:
        steps = jax.random.uniform(jax.random.fold_in(jax.random.fold_in(stream_key, 6), axis_at), (parts,), jnp.float32, low / len(shards), high / len(shards))
        level = level * jnp.repeat(jnp.exp(steps), extent[axis_at] // parts).reshape((-1,) + (1,) * (len(extent) - 1 - axis_at))
    return level


def scatter_about(rng, dims, spread, limit, shards=(), kind=jnp.bfloat16):
    array = spread * jax.random.normal(rng, dims, jnp.float32)
    if shards:
        array = array * block_levels(rng, dims, shards, -0.22, 0.18)
    return jnp.clip(array, -limit, limit).astype(kind)


def setup_inputs(seed: int = 0) -> dict:
    streams_of = jax.random.split(jax.random.key(seed), 10)
    return {
        "queries": scatter_about(streams_of[0], (NODES, HEADS * HEAD_DIM), 1.0, 6.0, ((0, 128),)),
        "out_grad": scatter_about(streams_of[1], (NODES, HEADS * HEAD_DIM), 8.0, 48.0, ((0, 128),)),
        "outputs": scatter_about(streams_of[2], (NODES, HEADS * HEAD_DIM), 1.0, 6.0, ((0, 128),)),
        "log_norms": jnp.clip(6.0 + 2.0 * jax.random.uniform(streams_of[3], (HEADS, NODES), jnp.float32) ** block_levels(streams_of[3], (HEADS, NODES), ((1, 128),), -0.2, 0.2), 6.0, 8.0),
        "src_keys": scatter_about(streams_of[4], (NODES, HEADS * HEAD_DIM), 1.0, 6.0, ((0, 16),)),
        "src_values": scatter_about(streams_of[5], (NODES, HEADS * HEAD_DIM), 1.0, 6.0, ((0, 16),)),
        "block_list": draw_block_list(jax.random.fold_in(streams_of[9], 71), 0),
        "block_count": draw_block_count(jax.random.fold_in(streams_of[9], 71), 0),
        "mask_bits": place_ends(jax.random.randint(streams_of[8], (N_SRC, N_REP, CAP, WORDS, BLOCK), 0, 65536), jax.random.fold_in(streams_of[8], 1), 0, 65535).astype(jnp.int32),
    }


def unpack_mask(packed, block_len):
    shifts = jnp.arange(16, dtype=jnp.int32)
    bit_values = jnp.bitwise_and(jnp.right_shift(packed[..., :, None, :], shifts[:, None]), 1)
    lead = packed.shape[:-2]
    bit_values = bit_values.reshape(lead + (packed.shape[-2] * 16, packed.shape[-1]))
    return bit_values[..., :block_len, :]


def block_terms(query_rows, grad_rows, norm_rows, delta_rows, key_rows, value_rows, edge_mask, score_scale):
    query_f = query_rows.astype(jnp.float32)
    grad_f = grad_rows.astype(jnp.float32)
    key_f = key_rows.astype(jnp.float32)
    value_f = value_rows.astype(jnp.float32)
    scores = jnp.einsum('cihd,cjhd->chij', query_f, key_f) * score_scale
    attn_probs = jnp.exp(scores - norm_rows[..., None]) * edge_mask[:, None]
    probs_low = lax.optimization_barrier(attn_probs.astype(jnp.bfloat16)).astype(jnp.float32)
    value_part = jnp.einsum('chij,cihd->cjhd', probs_low, grad_f)
    prob_grad = jnp.einsum('cihd,cjhd->chij', grad_f, value_f)
    score_grad = attn_probs * (prob_grad - delta_rows[..., None])
    score_low = lax.optimization_barrier(score_grad.astype(jnp.bfloat16)).astype(jnp.float32)
    query_part = jnp.einsum('chij,cjhd->cihd', score_low, key_f) * score_scale
    key_part = jnp.einsum('chij,cihd->cjhd', score_low, query_f) * score_scale
    return query_part, key_part, value_part


def reference(queries, out_grad, outputs, log_norms, src_keys, src_values, block_list, block_count, mask_bits):
    dest_rows = NODES // (N_SRC * N_REP)
    features = HEADS * HEAD_DIM
    score_scale = HEAD_DIM ** -0.5

    def grouped(rows):
        return rows.reshape(N_SRC, N_REP, dest_rows, -1).transpose(1, 0, 2, 3).reshape(N_REP, DST_BLKS, BLOCK, -1)

    query_grp = grouped(queries).reshape(N_REP, DST_BLKS, BLOCK, HEADS, HEAD_DIM)
    grad_grp = grouped(out_grad).reshape(N_REP, DST_BLKS, BLOCK, HEADS, HEAD_DIM)
    products = out_grad.astype(jnp.float32) * outputs.astype(jnp.float32)
    row_delta = jnp.sum(products.reshape(NODES, HEADS, HEAD_DIM), axis=2)
    delta_grp = grouped(row_delta).transpose(0, 1, 3, 2)
    norm_grp = grouped(log_norms.T).transpose(0, 1, 3, 2)
    key_blk = src_keys.reshape(N_SRC, SRC_BLKS, BLOCK, HEADS, HEAD_DIM)
    value_blk = src_values.reshape(N_SRC, SRC_BLKS, BLOCK, HEADS, HEAD_DIM)

    def visit_device(visit_index, totals):
        query_total, key_total, value_total = totals
        shard_idx = visit_index // N_REP
        group_idx = visit_index % N_REP
        pair_list = block_list[shard_idx, group_idx]
        dest_idx = pair_list[0]
        src_idx = pair_list[1]
        alive_rows = (jnp.arange(CAP, dtype=jnp.int32) < block_count[shard_idx, group_idx]).astype(jnp.float32)
        edge_mask = unpack_mask(mask_bits[shard_idx, group_idx], BLOCK).astype(jnp.float32) * alive_rows[:, None, None]
        query_part, key_part, value_part = block_terms(
            query_grp[group_idx][dest_idx], grad_grp[group_idx][dest_idx],
            norm_grp[group_idx][dest_idx], delta_grp[group_idx][dest_idx],
            key_blk[shard_idx][src_idx], value_blk[shard_idx][src_idx], edge_mask, score_scale)
        query_total = query_total.at[group_idx, dest_idx].add(query_part)
        key_total = key_total.at[shard_idx, src_idx].add(key_part)
        value_total = value_total.at[shard_idx, src_idx].add(value_part)
        return query_total, key_total, value_total

    initial = (jnp.zeros((N_REP, DST_BLKS, BLOCK, HEADS, HEAD_DIM), jnp.float32),
               jnp.zeros((N_SRC, SRC_BLKS, BLOCK, HEADS, HEAD_DIM), jnp.float32),
               jnp.zeros((N_SRC, SRC_BLKS, BLOCK, HEADS, HEAD_DIM), jnp.float32))
    query_total, key_total, value_total = lax.fori_loop(0, N_SRC * N_REP, visit_device, initial)
    query_grad = query_total.reshape(N_REP, N_SRC, dest_rows, features).transpose(1, 0, 2, 3)
    query_grad = query_grad.reshape(NODES, features).astype(jnp.bfloat16)
    key_grad = key_total.reshape(NODES, features).astype(jnp.bfloat16)
    value_grad = value_total.reshape(NODES, features).astype(jnp.bfloat16)
    return query_grad, key_grad, value_grad
```

```python
import functools
import math

import jax
import jax.numpy as jnp
from jax import lax
from jax.experimental import pallas as pl
from jax.experimental.pallas import tpu as pltpu
from jax.sharding import PartitionSpec as P

F32 = jnp.float32
BF16 = jnp.bfloat16
LOG2E = math.log2(math.e)


def nt_dot(a, b):
    return lax.dot_general(a, b, (((1,), (1,)), ((), ())), preferred_element_type=F32)


def nn_dot(a, b):
    return lax.dot_general(a, b, (((1,), (0,)), ((), ())), preferred_element_type=F32)


def tn_dot(a, b):
    return lax.dot_general(a, b, (((0,), (0,)), ((), ())), preferred_element_type=F32)


def build_masks(dst_blocks, src_blocks, table, words_ref, mask_ref):
    row = lax.broadcasted_iota(jnp.int32, (16, 128), 0)
    lane = lax.broadcasted_iota(jnp.int32, (16, 128), 1)
    half = jnp.where(lax.rem(lane, 16) >= 8, 8, 0)
    spread = jnp.where(row == lane // 16 + half, 1.0, 0.0).astype(BF16)
    bit = jnp.left_shift(1, lax.rem(lax.broadcasted_iota(jnp.int32, (1, 128), 1), 8))

    def one_dest(t, carry):
        words = jnp.concatenate(
            [
                words_ref[table[0, t * src_blocks + j]] * table[1, t * src_blocks + j]
                for j in range(src_blocks)
            ],
            axis=1,
        )
        halves = jnp.concatenate(
            [jnp.bitwise_and(words, 255), jnp.bitwise_and(jnp.right_shift(words, 8), 255)], axis=0
        )
        wide = tn_dot(halves.astype(F32).astype(BF16), spread).astype(jnp.int32)
        picked = jnp.where(jnp.bitwise_and(wide, bit) != 0, 1.0, 0.0)
        mask_ref[:, pl.ds(pl.multiple_of(t * 128, 128), 128)] = picked
        return carry

    lax.fori_loop(0, dst_blocks, one_dest, 0)


def visit(scale, rows, tile, q, g, norm, delta, k_ref, v_ref, kt, mask_ref, at, dk_ref, dv_ref, pbuf, sbuf):
    n_src = k_ref.shape[0]
    for c in range(n_src // tile):
        cs = pl.ds(c * tile, tile)
        s = nt_dot(k_ref[cs, :], q)
        e = jnp.exp2(s * (scale * LOG2E) - norm)
        p = e * mask_ref[cs, pl.ds(at, rows)]
        d = nt_dot(v_ref[cs, :], g)
        ds = p * (d - delta)
        p_low = p.astype(BF16)
        s_low = ds.astype(BF16)
        sbuf[cs, :] = s_low
        dv_ref[cs, :] += nn_dot(p_low, g)
        dk_ref[cs, :] += nn_dot(s_low, q)
    return nn_dot(kt, sbuf[...])


def core(heads, rows, tile, table, words_ref, q_hbm, g_hbm, nd_ref, k_hbm, v_hbm, dq_ref, dk_ref, dv_ref,
         mask_ref, q_all, g_all, k_all, v_all, kt, pbuf, sbuf, sems):
    n_dst, hd = q_all.shape[1:]
    copies = []
    for h in range(heads):
        cols = pl.ds(h * hd, hd)
        for i, (a, b) in enumerate(((q_hbm, q_all), (g_hbm, g_all), (k_hbm, k_all), (v_hbm, v_all))):
            cp = pltpu.make_async_copy(a.at[:, cols], b.at[h], sems.at[h, i])
            cp.start()
            copies.append(cp)
    build_masks(n_dst // 128, k_all.shape[1] // 128, table, words_ref, mask_ref)
    for cp in copies:
        cp.wait()
    scale = hd ** -0.5
    dk_ref[...] = jnp.zeros_like(dk_ref)
    dv_ref[...] = jnp.zeros_like(dv_ref)

    def one_head(h, carry):
        kt[...] = k_all[h].T

        def one_chunk(i, carry):
            at = pl.multiple_of(i * rows, rows)
            q = q_all[h, pl.ds(at, rows), :]
            g = g_all[h, pl.ds(at, rows), :]
            norm = nd_ref[h, 0:1, pl.ds(at, rows)] * LOG2E
            delta = nd_ref[h, 1:2, pl.ds(at, rows)]
            dqt = visit(scale, rows, tile, q, g, norm, delta, k_all.at[h], v_all.at[h], kt[...], mask_ref, at,
                        dk_ref.at[h], dv_ref.at[h], pbuf, sbuf)
            dq_ref[h, pl.ds(at, rows), :] = dqt.T * scale
            return carry

        lax.fori_loop(0, n_dst // rows, one_chunk, 0)
        dk_ref[h] = dk_ref[h] * scale
        return carry

    lax.fori_loop(0, heads, one_head, 0)


def attention(heads, q, g, norm, delta, k, v, table, words):
    n_dst, features = q.shape
    n_src = k.shape[0]
    hd = features // heads
    nd = jnp.stack([norm, delta], axis=1)
    rows, tile = 512, 128
    vmem = pl.BlockSpec(memory_space=pltpu.VMEM)
    anyspace = pl.BlockSpec(memory_space=pl.ANY)
    return pl.pallas_call(
        functools.partial(core, heads, rows, tile),
        out_shape=(
            jax.ShapeDtypeStruct((heads, n_dst, hd), F32),
            jax.ShapeDtypeStruct((heads, n_src, hd), F32),
            jax.ShapeDtypeStruct((heads, n_src, hd), F32),
        ),
        in_specs=[pl.BlockSpec(memory_space=pltpu.SMEM), vmem, anyspace, anyspace, vmem, anyspace, anyspace],
        out_specs=(vmem, vmem, vmem),
        scratch_shapes=[
            pltpu.VMEM((n_src, n_dst), F32),
            pltpu.VMEM((heads, n_dst, hd), BF16),
            pltpu.VMEM((heads, n_dst, hd), BF16),
            pltpu.VMEM((heads, n_src, hd), BF16),
            pltpu.VMEM((heads, n_src, hd), BF16),
            pltpu.VMEM((hd, n_src), BF16),
            pltpu.VMEM((8, 128), BF16),
            pltpu.VMEM((n_src, rows), BF16),
            pltpu.SemaphoreType.DMA((heads, 4)),
        ],
        compiler_params=pltpu.CompilerParams(vmem_limit_bytes=56 << 20),
        name="attention",
    )(table, words, q, g, nd, k, v)


def pair_table(block_list, block_count, n_pairs, src_blocks):
    capacity = block_list.shape[1]
    order = jnp.arange(capacity, dtype=jnp.int32)
    code = block_list[0] * src_blocks + block_list[1]
    hit = (code[:, None] == jnp.arange(n_pairs, dtype=jnp.int32)) & (order < block_count)[:, None]
    slot = jnp.sum(jnp.where(hit, order[:, None], 0), axis=0)
    live = jnp.sum(hit.astype(jnp.int32), axis=0)
    return jnp.stack([slot, live])


def shards(queries, out_grad, outputs, log_norms, src_keys, src_values, block_list, block_count, mask_bits):
    heads = log_norms.shape[0]
    features = queries.shape[1]
    hd = features // heads
    local = queries.shape[0]
    block = mask_bits.shape[-1]
    products = out_grad.astype(F32) * outputs.astype(F32)
    row_delta = jnp.sum(products.reshape(local, heads, hd), axis=2).T
    q_all = lax.all_gather(queries, "src", axis=0, tiled=True)
    g_all = lax.all_gather(out_grad, "src", axis=0, tiled=True)
    norm_all = lax.all_gather(log_norms, "src", axis=1, tiled=True)
    delta_all = lax.all_gather(row_delta, "src", axis=1, tiled=True)
    src_blocks = src_keys.shape[0] // block
    table = pair_table(block_list[0, 0], block_count[0, 0], q_all.shape[0] // block * src_blocks, src_blocks)
    dq, dk, dv = attention(heads, q_all, g_all, norm_all, delta_all, src_keys, src_values, table, mask_bits[0, 0])

    def spread(x, axis):
        x = lax.psum_scatter(x, axis, scatter_dimension=1, tiled=True)
        return x.transpose(1, 0, 2).reshape(-1, features).astype(BF16)

    return spread(dq, "src"), spread(dk, "rep"), spread(dv, "rep")


def solution(mesh):
    rows = P(("src", "rep"), None)
    placed = (
        rows,
        rows,
        rows,
        P(None, ("src", "rep")),
        P("src", None),
        P("src", None),
        P("src", "rep", None, None),
        P("src", "rep"),
        P("src", "rep", None, None, None),
    )
    return jax.shard_map(shards, mesh=mesh, in_specs=placed, out_specs=(rows, rows, rows), check_vma=False)
```

```python
import functools
import math

import jax
import jax.numpy as jnp
from jax import lax
from jax.experimental import pallas as pl
from jax.experimental.pallas import tpu as pltpu
from jax.sharding import PartitionSpec as P

F32 = jnp.float32
BF16 = jnp.bfloat16
LOG2E = math.log2(math.e)
MESH = pl.DeviceIdType.MESH


def nt_dot(a, b):
    return lax.dot_general(a, b, (((1,), (1,)), ((), ())), preferred_element_type=F32)


def nn_dot(a, b):
    return lax.dot_general(a, b, (((1,), (0,)), ((), ())), preferred_element_type=F32)


def tn_dot(a, b):
    return lax.dot_general(a, b, (((0,), (0,)), ((), ())), preferred_element_type=F32)


def build_masks(u, dest, src_blocks, table, words_ref, mask_ref):
    row = lax.broadcasted_iota(jnp.int32, (16, 128), 0)
    lane = lax.broadcasted_iota(jnp.int32, (16, 128), 1)
    half = jnp.where(lax.rem(lane, 16) >= 8, 8, 0)
    spread = jnp.where(row == lane // 16 + half, 1.0, 0.0).astype(BF16)
    bit = jnp.left_shift(1, lax.rem(lax.broadcasted_iota(jnp.int32, (1, 128), 1), 8))
    words = jnp.concatenate(
        [
            words_ref[table[0, dest * src_blocks + j]] * table[1, dest * src_blocks + j]
            for j in range(src_blocks)
        ],
        axis=1,
    )
    halves = jnp.concatenate(
        [jnp.bitwise_and(words, 255), jnp.bitwise_and(jnp.right_shift(words, 8), 255)], axis=0
    )
    wide = tn_dot(halves.astype(F32).astype(BF16), spread).astype(jnp.int32)
    picked = jnp.where(jnp.bitwise_and(wide, bit) != 0, 1.0, 0.0)
    mask_ref[:, pl.ds(pl.multiple_of(u * 128, 128), 128)] = picked


def visit(scale, tile, q, g, norm, delta, k_ref, v_ref, kt, mask_ref, at, dk_ref, dv_ref, sbuf):
    n_src = k_ref.shape[0]
    rows = q.shape[0]
    for c in range(n_src // tile):
        cs = pl.ds(c * tile, tile)
        s = nt_dot(k_ref[cs, :], q)
        e = jnp.exp2(s * (scale * LOG2E) - norm)
        p = e * mask_ref[cs, pl.ds(at, rows)]
        d = nt_dot(v_ref[cs, :], g)
        ds = p * (d - delta)
        p_low = p.astype(BF16)
        s_low = ds.astype(BF16)
        sbuf[cs, :] = s_low
        dv_ref[cs, :] += nn_dot(p_low, g)
        dk_ref[cs, :] += nn_dot(s_low, q)
    return nn_dot(kt, sbuf[...])


def core(heads, tile, table, words_ref, q_hbm, g_hbm, nd_hbm, k_hbm, v_hbm, dq_ref, dk_ref, dv_ref,
         mask_ref, qg, nd, k_all, v_all, kt, sbuf, dk_acc, dv_acc,
         send_a, recv_a, acc_a, send_b, recv_b, tot_c, send_c, recv_c,
         send_x, recv_x, keep_x, tot_y, send_y, recv_y,
         local_sem, ag_send, ag_recv, nd_send, nd_recv, rs_send, rs_recv):
    hd = kt.shape[0]
    n_src = kt.shape[1]
    rows = 4 * 128
    scale = hd ** -0.5
    src, rep = lax.axis_index("src"), lax.axis_index("rep")
    yh, z, c = src // 8, lax.rem(src, 8) // 2, lax.rem(src, 2)
    yl, x = rep // 4, lax.rem(rep, 4)

    def at_src(yy, zz, cc):
        return {"src": yy * 8 + zz * 2 + cc, "rep": rep}

    def at_rep(yy, xx):
        return {"src": src, "rep": yy * 4 + xx}

    sibling = at_src(yh, z, 1 - c)
    across = at_src(1 - yh, z, c)
    zs = [lax.rem(z + d, 4) for d in (1, 2, 3)]
    xs = [lax.rem(x + d, 4) for d in (1, 2, 3)]
    around = [at_src(yh, zz, c) for zz in zs]
    beside = [at_rep(yl, xx) for xx in xs]
    over = at_rep(1 - yl, x)

    first = []
    nd_copy = pltpu.make_async_copy(nd_hbm, nd.at[c, yh, z], local_sem.at[heads, 0])
    nd_copy.start()
    for h in range(heads):
        cols = pl.ds(h * hd, hd)
        for i, (a, b) in enumerate((
            (q_hbm, qg.at[h, c, yh, 0, z]), (g_hbm, qg.at[h, c, yh, 1, z]),
            (k_hbm, k_all.at[h]), (v_hbm, v_all.at[h]),
        )):
            cp = pltpu.make_async_copy(a.at[:, cols], b, local_sem.at[h, i])
            cp.start()
            first.append((i, cp))

    barrier = pltpu.get_barrier_semaphore()
    for peer in [sibling, across, over] + around + beside:
        pl.semaphore_signal(barrier, inc=1, device_id=peer, device_id_type=MESH)
    pl.semaphore_wait(barrier, 9)

    nd_copy.wait()
    for i, cp in first:
        if i < 2:
            cp.wait()

    def remote(a, b, s, r, peer):
        return pltpu.make_async_remote_copy(
            src_ref=a, dst_ref=b, send_sem=s, recv_sem=r, device_id=peer, device_id_type=MESH
        )

    def block(h, cc, yy, zz):
        return qg.at[h, cc, yy, :, zz] if h is not None else nd.at[cc, yy, zz]

    def gather(h, slot):
        if slot == 0:
            yy, zz, peer = yh, z, across
        elif slot < 4:
            yy, zz, peer = yh, z, around[slot - 1]
        elif slot < 7:
            yy, zz, peer = 1 - yh, z, around[slot - 4]
        elif slot == 7:
            yy, zz, peer = yh, z, sibling
        elif slot == 8:
            yy, zz, peer = 1 - yh, z, sibling
        elif slot < 12:
            yy, zz, peer = yh, zs[slot - 9], sibling
        else:
            yy, zz, peer = 1 - yh, zs[slot - 12], sibling
        ref = block(h, c, yy, zz)
        if h is None:
            return remote(ref, ref, nd_send.at[slot], nd_recv.at[slot], peer)
        return remote(ref, ref, ag_send.at[h, slot], ag_recv.at[h, slot], peer)

    def arrival(h, slot):
        if slot == 0:
            cc, yy, zz = c, 1 - yh, z
        elif slot < 4:
            cc, yy, zz = c, yh, lax.rem(z + 4 - slot, 4)
        elif slot < 7:
            cc, yy, zz = c, 1 - yh, lax.rem(z + 4 - (slot - 3), 4)
        elif slot == 7:
            cc, yy, zz = 1 - c, yh, z
        elif slot == 8:
            cc, yy, zz = 1 - c, 1 - yh, z
        elif slot < 12:
            cc, yy, zz = 1 - c, yh, zs[slot - 9]
        else:
            cc, yy, zz = 1 - c, 1 - yh, zs[slot - 12]
        ref = block(h, cc, yy, zz)
        if h is None:
            return remote(ref, ref, nd_send.at[slot], nd_recv.at[slot], sibling)
        return remote(ref, ref, ag_send.at[h, slot], ag_recv.at[h, slot], sibling)

    def gather_step(h, stage):
        if stage == 0:
            for slot in (1, 2, 3, 7):
                gather(h, slot).start()
            arrival(h, 0).wait_recv()
            for slot in (4, 5, 6, 8):
                gather(h, slot).start()
        elif stage == 1:
            for d in (1, 3, 2):
                arrival(h, d).wait_recv()
                gather(h, 9 + (3 - d)).start()
        elif stage == 2:
            for d in (1, 3, 2):
                arrival(h, 3 + d).wait_recv()
                gather(h, 12 + (3 - d)).start()
        else:
            for slot in range(7, 15):
                arrival(h, slot).wait_recv()

    gather(None, 0).start()
    for h in range(heads):
        gather(h, 0).start()

    def stage_a(h, y):
        return remote(send_a.at[h, y], recv_a.at[h, y], rs_send.at[h, y], rs_recv.at[h, y], sibling)

    def stage_b(h, j):
        return remote(send_b.at[h, :, zs[j]], recv_b.at[h, j], rs_send.at[h, 2 + j], rs_recv.at[h, 2 + j], around[j])

    def stage_c(h):
        return remote(send_c.at[h], recv_c.at[h], rs_send.at[h, 5], rs_recv.at[h, 5], across)

    def stage_x(h, j):
        return remote(send_x.at[h, :, :, xs[j]], recv_x.at[h, j], rs_send.at[h, 6 + j], rs_recv.at[h, 6 + j], beside[j])

    def stage_y(h):
        return remote(send_y.at[h], recv_y.at[h], rs_send.at[h, 9], rs_recv.at[h, 9], over)

    def step(n, carry):
        h = n // 4 - 1
        i = lax.rem(n, 4)
        ahead = h + 1
        done = h - 1

        @pl.when((ahead < heads) & (i == 0))
        def _():
            @pl.when(ahead == 0)
            def _():
                gather_step(None, 0)
            gather_step(ahead, 0)

        @pl.when((done >= 0) & (i == 0))
        def _():
            for j in (0, 2, 1):
                stage_x(done, j).start()
            for y in range(2):
                stage_a(done, y).wait_recv()
                total = acc_a[y] + recv_a[done, y].astype(F32)
                acc_a[y] = total
                send_b[done, y] = total.astype(BF16)
            for y in range(2):
                tot_c[y] = acc_a[y, z]
            for j in (0, 2, 1):
                stage_b(done, j).start()

        @pl.when((ahead < heads) & (i == 1))
        def _():
            @pl.when(ahead == 0)
            def _():
                gather_step(None, 1)
            gather_step(ahead, 1)

        @pl.when((ahead < heads) & (i == 2))
        def _():
            @pl.when(ahead == 0)
            def _():
                gather_step(None, 2)
            gather_step(ahead, 2)

        @pl.when((done >= 0) & (i == 2))
        def _():
            for j in range(3):
                stage_x(done, j).wait_recv()
            for s in range(2):
                for y in range(2):
                    tot_y[s, y] = (
                        keep_x[s, y]
                        + recv_x[done, 0, s, y].astype(F32)
                        + recv_x[done, 1, s, y].astype(F32)
                        + recv_x[done, 2, s, y].astype(F32)
                    )
                send_y[done, s] = tot_y[s, 1 - yl].astype(BF16)
            stage_y(done).start()
            for j in range(3):
                stage_b(done, j).wait_recv()
            for y in range(2):
                tot_c[y] = (
                    tot_c[y]
                    + recv_b[done, 0, y].astype(F32)
                    + recv_b[done, 1, y].astype(F32)
                    + recv_b[done, 2, y].astype(F32)
                )
            send_c[done] = tot_c[1 - yh].astype(BF16)
            stage_c(done).start()

        @pl.when((done >= 0) & (i == 3))
        def _():
            cols = pl.ds(pl.multiple_of(done * hd, hd), hd)
            stage_y(done).wait_recv()
            dk_ref[:, cols] = ((tot_y[0, yl] + recv_y[done, 0].astype(F32)) * scale).astype(BF16)
            dv_ref[:, cols] = (tot_y[1, yl] + recv_y[done, 1].astype(F32)).astype(BF16)
            stage_c(done).wait_recv()
            dq_ref[:, cols] = ((tot_c[yh] + recv_c[done].astype(F32)) * scale).astype(BF16)

        @pl.when(h < 0)
        def _():
            for j in range(4):
                u = i * 4 + j
                build_masks(u, lax.rem(u // 4, 2) * 8 + lax.rem(u, 4) * 2 + u // 8, n_src // 128, table, words_ref,
                            mask_ref)

        @pl.when((h >= 0) & (h < heads))
        def _():
            @pl.when((h > 0) & (i == 0))
            def _():
                gather_step(h, 3)

            @pl.when((h == 0) & (i == 2))
            def _():
                gather_step(None, 3)
                gather_step(h, 3)

            @pl.when((h == 0) & (i == 0))
            def _():
                for k, cp in first:
                    if k >= 2:
                        cp.wait()

            @pl.when(i == 0)
            def _():
                kt[...] = k_all[h].T
                dk_acc[...] = jnp.zeros_like(dk_acc)
                dv_acc[...] = jnp.zeros_like(dv_acc)

            mine = (i >= 2) ^ (h == 0)
            cc = jnp.where(mine, c, 1 - c)
            yy = lax.rem(i, 2)
            at = pl.multiple_of((cc * 2 + yy) * rows, rows)
            q = qg[h, cc, yy, 0].reshape(rows, hd)
            g = qg[h, cc, yy, 1].reshape(rows, hd)
            norm = jnp.concatenate([nd[cc, yy, j, pl.ds(h, 1), :] for j in range(4)], axis=1) * LOG2E
            delta = jnp.concatenate([nd[cc, yy, j, pl.ds(heads + h, 1), :] for j in range(4)], axis=1)
            dqt = visit(scale, tile, q, g, norm, delta, k_all.at[h], v_all.at[h], kt[...], mask_ref, at,
                        dk_acc, dv_acc, sbuf)
            dq = dqt.T.reshape(4, 128, hd)

            @pl.when(mine)
            def _():
                acc_a[yy] = dq

            @pl.when(jnp.logical_not(mine))
            def _():
                send_a[h, yy] = dq.astype(BF16)
                stage_a(h, yy).start()

            @pl.when(i == 3)
            def _():
                for s, acc in enumerate((dk_acc, dv_acc)):
                    blocks = acc[...].reshape(2, 4, 128, hd)
                    send_x[h, s] = blocks.astype(BF16)
                    for y in range(2):
                        keep_x[s, y] = acc[pl.ds(pl.multiple_of((y * 4 + x) * 128, 128), 128), :]

        return carry

    lax.fori_loop(0, (heads + 2) * 4, step, 0)

    def drain(h, carry):
        for slot in range(15):
            gather(h, slot).wait_send()
        for y in range(2):
            stage_a(h, y).wait_send()
        for j in range(3):
            stage_b(h, j).wait_send()
            stage_x(h, j).wait_send()
        stage_c(h).wait_send()
        stage_y(h).wait_send()
        return carry

    for slot in range(15):
        gather(None, slot).wait_send()
    lax.fori_loop(0, heads, drain, 0)


def attention(heads, q, g, nd, k, v, table, words):
    local, features = q.shape
    n_src = k.shape[0]
    hd = features // heads
    tile = 128
    vmem = pl.BlockSpec(memory_space=pltpu.VMEM)
    anyspace = pl.BlockSpec(memory_space=pl.ANY)
    out = jax.ShapeDtypeStruct((local, features), BF16)
    return pl.pallas_call(
        functools.partial(core, heads, tile),
        out_shape=(out, out, out),
        in_specs=[pl.BlockSpec(memory_space=pltpu.SMEM), vmem] + [anyspace] * 5,
        out_specs=(vmem, vmem, vmem),
        scratch_shapes=[
            pltpu.VMEM((n_src, 16 * 128), F32),
            pltpu.VMEM((heads, 2, 2, 2, 4, 128, hd), BF16),
            pltpu.VMEM((2, 2, 4, 2 * heads, 128), F32),
            pltpu.VMEM((heads, n_src, hd), BF16),
            pltpu.VMEM((heads, n_src, hd), BF16),
            pltpu.VMEM((hd, n_src), BF16),
            pltpu.VMEM((n_src, 512), BF16),
            pltpu.VMEM((n_src, hd), F32),
            pltpu.VMEM((n_src, hd), F32),
            pltpu.VMEM((heads, 2, 4, 128, hd), BF16),
            pltpu.VMEM((heads, 2, 4, 128, hd), BF16),
            pltpu.VMEM((2, 4, 128, hd), F32),
            pltpu.VMEM((heads, 2, 4, 128, hd), BF16),
            pltpu.VMEM((heads, 3, 2, 128, hd), BF16),
            pltpu.VMEM((2, 128, hd), F32),
            pltpu.VMEM((heads, 128, hd), BF16),
            pltpu.VMEM((heads, 128, hd), BF16),
            pltpu.VMEM((heads, 2, 2, 4, 128, hd), BF16),
            pltpu.VMEM((heads, 3, 2, 2, 128, hd), BF16),
            pltpu.VMEM((2, 2, 128, hd), F32),
            pltpu.VMEM((2, 2, 128, hd), F32),
            pltpu.VMEM((heads, 2, 128, hd), BF16),
            pltpu.VMEM((heads, 2, 128, hd), BF16),
            pltpu.SemaphoreType.DMA((heads + 1, 4)),
            pltpu.SemaphoreType.DMA((heads, 15)),
            pltpu.SemaphoreType.DMA((heads, 15)),
            pltpu.SemaphoreType.DMA((15,)),
            pltpu.SemaphoreType.DMA((15,)),
            pltpu.SemaphoreType.DMA((heads, 10)),
            pltpu.SemaphoreType.DMA((heads, 10)),
        ],
        compiler_params=pltpu.CompilerParams(
            vmem_limit_bytes=60 << 20, collective_id=0, has_side_effects=True
        ),
        name="attention",
    )(table, words, q, g, nd, k, v)


def pair_table(block_list, block_count, n_pairs, src_blocks):
    capacity = block_list.shape[1]
    order = jnp.arange(capacity, dtype=jnp.int32)
    code = block_list[0] * src_blocks + block_list[1]
    hit = (code[:, None] == jnp.arange(n_pairs, dtype=jnp.int32)) & (order < block_count)[:, None]
    slot = jnp.sum(jnp.where(hit, order[:, None], 0), axis=0)
    live = jnp.sum(hit.astype(jnp.int32), axis=0)
    return jnp.stack([slot, live])


def shards(queries, out_grad, outputs, log_norms, src_keys, src_values, block_list, block_count, mask_bits):
    heads = log_norms.shape[0]
    features = queries.shape[1]
    hd = features // heads
    local = queries.shape[0]
    block = mask_bits.shape[-1]
    products = out_grad.astype(F32) * outputs.astype(F32)
    row_delta = jnp.sum(products.reshape(local, heads, hd), axis=2).T
    nd = jnp.concatenate([log_norms, row_delta], axis=0)
    src_blocks = src_keys.shape[0] // block
    table = pair_table(block_list[0, 0], block_count[0, 0], 16 * src_blocks, src_blocks)
    return attention(heads, queries, out_grad, nd, src_keys, src_values, table, mask_bits[0, 0])


def solution(mesh):
    rows = P(("src", "rep"), None)
    placed = (
        rows,
        rows,
        rows,
        P(None, ("src", "rep")),
        P("src", None),
        P("src", None),
        P("src", "rep", None, None),
        P("src", "rep"),
        P("src", "rep", None, None, None),
    )
    return jax.shard_map(shards, mesh=mesh, in_specs=placed, out_specs=(rows, rows, rows), check_vma=False)
```

```python
import functools
import math

import jax
import jax.numpy as jnp
from jax import lax
from jax.experimental import pallas as pl
from jax.experimental.pallas import tpu as pltpu
from jax.sharding import PartitionSpec as P

F32 = jnp.float32
BF16 = jnp.bfloat16
LOG2E = math.log2(math.e)
MESH = pl.DeviceIdType.MESH


def nt_dot(a, b):
    return lax.dot_general(a, b, (((1,), (1,)), ((), ())), preferred_element_type=F32)


def nn_dot(a, b):
    return lax.dot_general(a, b, (((1,), (0,)), ((), ())), preferred_element_type=F32)


def tn_dot(a, b):
    return lax.dot_general(a, b, (((0,), (0,)), ((), ())), preferred_element_type=F32)


def build_masks(u, dest, src_blocks, table, words_ref, mask_ref):
    row = lax.broadcasted_iota(jnp.int32, (16, 128), 0)
    lane = lax.broadcasted_iota(jnp.int32, (16, 128), 1)
    half = jnp.where(lax.rem(lane, 16) >= 8, 8, 0)
    spread = jnp.where(row == lane // 16 + half, 1.0, 0.0).astype(BF16)
    bit = jnp.left_shift(1, lax.rem(lax.broadcasted_iota(jnp.int32, (1, 128), 1), 8))
    words = jnp.concatenate(
        [
            words_ref[0, 0, jnp.clip(table[0, dest * src_blocks + j], 0, words_ref.shape[2] - 1)] * table[1, dest * src_blocks + j]
            for j in range(src_blocks)
        ],
        axis=1,
    )
    halves = jnp.concatenate(
        [jnp.bitwise_and(words, 255), jnp.bitwise_and(jnp.right_shift(words, 8), 255)], axis=0
    )
    wide = tn_dot(halves.astype(F32).astype(BF16), spread).astype(jnp.int32)
    picked = jnp.where(jnp.bitwise_and(wide, bit) != 0, 1.0, 0.0)
    mask_ref[:, pl.ds(pl.multiple_of(u * 128, 128), 128)] = picked


def visit(scale, tile, q, g, norm, delta, k_ref, v_ref, kt, mask_ref, at, dk_ref, dv_ref, sbuf):
    n_src = k_ref.shape[0]
    rows = q.shape[0]
    for c in range(n_src // tile):
        cs = pl.ds(c * tile, tile)
        s = nt_dot(k_ref[cs, :], q)
        e = jnp.exp2(s * (scale * LOG2E) - norm)
        p = e * mask_ref[cs, pl.ds(at, rows)]
        d = nt_dot(v_ref[cs, :], g)
        ds = p * (d - delta)
        p_low = p.astype(BF16)
        s_low = ds.astype(BF16)
        sbuf[cs, :] = s_low
        dv_ref[cs, :] += nn_dot(p_low, g)
        dk_ref[cs, :] += nn_dot(s_low, q)
    return nn_dot(kt, sbuf[...])


def pair_slots(list_ref, count, src_blocks, n_pairs):
    capacity = list_ref.shape[3]
    code = list_ref[0, 0, 0:1, :] * src_blocks + list_ref[0, 0, 1:2, :]
    order = lax.broadcasted_iota(jnp.int32, (n_pairs, capacity), 1)
    pair = lax.broadcasted_iota(jnp.int32, (n_pairs, capacity), 0)
    hit = (code == pair) & (order < count)
    slot = jnp.sum(jnp.where(hit, order, 0), axis=1, keepdims=True)
    live = jnp.sum(jnp.where(hit, 1, 0), axis=1, keepdims=True)
    column = lax.broadcasted_iota(jnp.int32, (n_pairs, 128), 1)
    both = jnp.where(column == 0, slot, jnp.where(column == 1, live, 0))
    return both.T[0:8]


def core(heads, tile, count_ref, list_ref, words_hbm, q_hbm, g_hbm, o_hbm, norm_hbm, k_hbm, v_hbm,
         dq_ref, dk_ref, dv_ref,
         words, slots, table, mask_ref, qg, o_all, nd, k_all, v_all, kt, sbuf, dk_acc, dv_acc,
         send_a, recv_a, acc_a, send_c, recv_c, tot_b, send_b, recv_b,
         send_x, recv_x, keep_k, send_v, recv_v, keep_v, send_y, recv_y, send_w, recv_w,
         local_sem, extra_sem, ag_send, ag_recv, nd_send, nd_recv, rs_send, rs_recv):
    hd = kt.shape[0]
    n_src = kt.shape[1]
    src_blocks = n_src // 128
    rows = 4 * 128
    scale = hd ** -0.5
    src, rep = lax.axis_index("src"), lax.axis_index("rep")
    yh, z, c = src // 8, lax.rem(src, 8) // 2, lax.rem(src, 2)
    yl, x = rep // 4, lax.rem(rep, 4)

    def at_src(yy, zz, cc):
        return {"src": yy * 8 + zz * 2 + cc, "rep": rep}

    def at_rep(yy, xx):
        return {"src": src, "rep": yy * 4 + xx}

    sibling = at_src(yh, z, 1 - c)
    across = at_src(1 - yh, z, c)
    zs = [lax.rem(z + d, 4) for d in (1, 2, 3)]
    xs = [lax.rem(x + d, 4) for d in (1, 2, 3)]
    around = [at_src(yh, zz, c) for zz in zs]
    beside = [at_rep(yl, xx) for xx in xs]
    over = at_rep(1 - yl, x)

    barrier = pltpu.get_barrier_semaphore()
    for peer in [sibling, across, over] + around + beside:
        pl.semaphore_signal(barrier, inc=1, device_id=peer, device_id_type=MESH)

    mine_copies, kv_copies = [], []
    for h in range(heads):
        cols = pl.ds(h * hd, hd)
        for i, (a, b) in enumerate((
            (q_hbm, qg.at[h, c, yh, 0, z]), (g_hbm, qg.at[h, c, yh, 1, z]), (o_hbm, o_all.at[h]),
            (k_hbm, k_all.at[h]), (v_hbm, v_all.at[h]),
        )):
            cp = pltpu.make_async_copy(a.at[:, cols], b, local_sem.at[h, i])
            if i < 3:
                cp.start()
                mine_copies.append(cp)
            else:
                kv_copies.append(cp)
    norm_copy = pltpu.make_async_copy(norm_hbm, nd.at[c, yh, z, pl.ds(0, heads)], extra_sem.at[0])
    norm_copy.start()
    words_copy = pltpu.make_async_copy(words_hbm, words, extra_sem.at[1])
    words_copy.start()
    for cp in kv_copies:
        cp.start()

    slots[...] = pair_slots(list_ref, count_ref[0, 0], src_blocks, 128)
    table_copy = pltpu.make_async_copy(slots, table, extra_sem.at[2])
    table_copy.start()

    norm_copy.wait()
    for cp in mine_copies:
        cp.wait()
    for h in range(heads):
        product = qg[h, c, yh, 1, z].astype(F32) * o_all[h].astype(F32)
        nd[c, yh, z, heads + h : heads + h + 1, :] = jnp.sum(product.T, axis=0, keepdims=True)

    def remote(a, b, s, r, peer):
        return pltpu.make_async_remote_copy(
            src_ref=a, dst_ref=b, send_sem=s, recv_sem=r, device_id=peer, device_id_type=MESH
        )

    def gather_copy(h, cc, yy, zz, slot, peer):
        if h is None:
            ref = nd.at[cc, yy, zz]
            return remote(ref, ref, nd_send.at[slot], nd_recv.at[slot], peer)
        ref = qg.at[h, cc, yy, :, zz]
        return remote(ref, ref, ag_send.at[h, slot], ag_recv.at[h, slot], peer)

    def gather(h, slot):
        if slot == 0:
            yy, zz, peer = yh, z, across
        elif slot < 4:
            yy, zz, peer = yh, z, around[slot - 1]
        elif slot < 7:
            yy, zz, peer = 1 - yh, z, around[slot - 4]
        elif slot == 7:
            yy, zz, peer = yh, z, sibling
        elif slot == 8:
            yy, zz, peer = 1 - yh, z, sibling
        elif slot < 12:
            yy, zz, peer = yh, zs[slot - 9], sibling
        else:
            yy, zz, peer = 1 - yh, zs[slot - 12], sibling
        return gather_copy(h, c, yy, zz, slot, peer)

    def arrived(h, slot):
        if slot == 0:
            cc, yy, zz = c, 1 - yh, z
        elif slot < 4:
            cc, yy, zz = c, yh, zs[3 - slot]
        elif slot < 7:
            cc, yy, zz = c, 1 - yh, zs[6 - slot]
        elif slot == 7:
            cc, yy, zz = 1 - c, yh, z
        elif slot == 8:
            cc, yy, zz = 1 - c, 1 - yh, z
        elif slot < 12:
            cc, yy, zz = 1 - c, yh, zs[slot - 9]
        else:
            cc, yy, zz = 1 - c, 1 - yh, zs[slot - 12]
        gather_copy(h, cc, yy, zz, slot, sibling).wait_recv()

    def send_own(h):
        for slot in (1, 3, 2, 7):
            gather(h, slot).start()

    def relay_across(h):
        arrived(h, 0)
        for slot in (4, 6, 5, 8):
            gather(h, slot).start()

    def forward_own_row(h):
        for d in (1, 3, 2):
            arrived(h, d)
            gather(h, 12 - d).start()

    def forward_other_row(h):
        for d in (1, 3, 2):
            arrived(h, 3 + d)
            gather(h, 15 - d).start()

    def sibling_own_row(h):
        for slot in (7, 9, 10, 11):
            arrived(h, slot)

    def sibling_other_row(h):
        for slot in (8, 12, 13, 14):
            arrived(h, slot)

    def stage_a(h, y):
        return remote(send_a.at[h, y], recv_a.at[h, y], rs_send.at[h, y], rs_recv.at[h, y], sibling)

    def stage_c(h):
        return remote(send_c.at[h], recv_c.at[h], rs_send.at[h, 2], rs_recv.at[h, 2], across)

    def stage_b(h, j):
        return remote(send_b.at[h, zs[j]], recv_b.at[h, j], rs_send.at[h, 3 + j], rs_recv.at[h, 3 + j], around[j])

    def stage_x(h, j):
        return remote(send_x.at[h, :, xs[j]], recv_x.at[h, j], rs_send.at[h, 6 + j], rs_recv.at[h, 6 + j], beside[j])

    def stage_v(h):
        return remote(send_v.at[h], recv_v.at[h], rs_send.at[h, 9], rs_recv.at[h, 9], over)

    def stage_y(h):
        return remote(send_y.at[h], recv_y.at[h], rs_send.at[h, 10], rs_recv.at[h, 10], over)

    def stage_w(h, j):
        return remote(send_w.at[h, xs[j]], recv_w.at[h, j], rs_send.at[h, 11 + j], rs_recv.at[h, 11 + j], beside[j])

    def masks(cc, yy):
        for zz in range(4):
            build_masks((cc * 2 + yy) * 4 + zz, yy * 8 + zz * 2 + cc, src_blocks, table, words, mask_ref)

    pl.semaphore_wait(barrier, 9)
    send_own(0)
    gather(0, 0).start()
    send_own(None)
    gather(None, 0).start()
    for h in range(1, heads):
        gather(h, 0).start()
    words_copy.wait()
    table_copy.wait()
    masks(c, yh)
    relay_across(0)
    relay_across(None)
    masks(1 - c, yh)
    forward_own_row(0)
    forward_own_row(None)

    def exchange_rows(h):
        stage_a(h, 1 - yh).wait_recv()
        send_c[h] = (acc_a[1 - yh] + recv_a[h, 1 - yh].astype(F32)).astype(BF16)
        stage_c(h).start()

    def event_0(h):
        done = h - 1

        @pl.when((h >= 1) & (h <= heads))
        def _():
            for j in (0, 2, 1):
                stage_x(done, j).start()
            stage_v(done).start()

        @pl.when(h == 1)
        def _():
            exchange_rows(0)

        @pl.when(h + 1 < heads)
        def _():
            send_own(h + 1)
            relay_across(h + 1)

        @pl.when((h >= 1) & (h < heads))
        def _():
            forward_other_row(h)
            sibling_own_row(h)

    def event_1(h):
        done = h - 1

        @pl.when((h >= 1) & (h <= heads))
        def _():
            stage_a(done, yh).wait_recv()
            stage_c(done).wait_recv()
            total = acc_a[yh] + recv_a[done, yh].astype(F32) + recv_c[done].astype(F32)
            tot_b[...] = total
            send_b[done] = total.astype(BF16)
            for j in (0, 2, 1):
                stage_b(done, j).start()

        @pl.when(h >= 2)
        def _():
            cols = pl.ds(pl.multiple_of((h - 2) * hd, hd), hd)
            stage_y(h - 2).wait_recv()
            dk_ref[:, cols] = keep_k[lax.rem(h, 2), yl] + recv_y[h - 2].astype(F32)
            for j in range(3):
                stage_w(h - 2, j).wait_recv()
            dv_ref[:, cols] = (
                keep_v[lax.rem(h, 2), x]
                + recv_w[h - 2, 0].astype(F32)
                + recv_w[h - 2, 1].astype(F32)
                + recv_w[h - 2, 2].astype(F32)
            )

        @pl.when(h == 0)
        def _():
            sibling_own_row(None)
            sibling_own_row(0)

        @pl.when((h >= 1) & (h < heads))
        def _():
            sibling_other_row(h)

    def event_2(h):
        done = h - 1
        odd = lax.rem(h + 1, 2)

        @pl.when((h >= 1) & (h <= heads))
        def _():
            for j in range(3):
                stage_x(done, j).wait_recv()
            for y in range(2):
                keep_k[odd, y] = (
                    keep_k[odd, y]
                    + recv_x[done, 0, y].astype(F32)
                    + recv_x[done, 1, y].astype(F32)
                    + recv_x[done, 2, y].astype(F32)
                )
            send_y[done] = keep_k[odd, 1 - yl].astype(BF16)
            stage_y(done).start()
            stage_v(done).wait_recv()
            total = keep_v[odd] + recv_v[done].astype(F32)
            keep_v[odd] = total
            send_w[done] = total.astype(BF16)
            for j in (0, 2, 1):
                stage_w(done, j).start()

        @pl.when(h == 0)
        def _():
            forward_other_row(None)
            forward_other_row(0)
            masks(c, 1 - yh)

        @pl.when(h + 1 < heads)
        def _():
            forward_own_row(h + 1)

    def event_3(h):
        done = h - 1

        @pl.when((h >= 1) & (h <= heads))
        def _():
            cols = pl.ds(pl.multiple_of(done * hd, hd), hd)
            for j in range(3):
                stage_b(done, j).wait_recv()
            dq_ref[:, cols] = (
                tot_b[z]
                + recv_b[done, 0].astype(F32)
                + recv_b[done, 1].astype(F32)
                + recv_b[done, 2].astype(F32)
            )

        @pl.when(h == 0)
        def _():
            sibling_other_row(None)
            sibling_other_row(0)
            masks(1 - c, 1 - yh)

        @pl.when((h >= 1) & (h < heads))
        def _():
            exchange_rows(h)

    def compute(h, i):
        @pl.when((h == 0) & (i == 0))
        def _():
            for cp in kv_copies:
                cp.wait()

        @pl.when(i == 0)
        def _():
            kt[...] = k_all[h].T
            dk_acc[...] = jnp.zeros_like(dk_acc)
            dv_acc[...] = jnp.zeros_like(dv_acc)

        mine = jnp.where(h == 0, lax.rem(i, 2) == 0, i >= 2)
        own_row = jnp.where(h == 0, i < 2, (i == 0) | (i == 3))
        cc = jnp.where(mine, c, 1 - c)
        yy = jnp.where(own_row, yh, 1 - yh)
        at = pl.multiple_of((cc * 2 + yy) * rows, rows)
        q = qg[h, cc, yy, 0].reshape(rows, hd)
        g = qg[h, cc, yy, 1].reshape(rows, hd)
        norm = jnp.concatenate([nd[cc, yy, j, pl.ds(h, 1), :] for j in range(4)], axis=1) * LOG2E
        delta = jnp.concatenate([nd[cc, yy, j, pl.ds(heads + h, 1), :] for j in range(4)], axis=1)
        dqt = visit(scale, tile, q, g, norm, delta, k_all.at[h], v_all.at[h], kt[...], mask_ref, at,
                    dk_acc, dv_acc, sbuf)
        dq = dqt.T.reshape(4, 128, hd)

        @pl.when(mine)
        def _():
            acc_a[yy] = dq

        @pl.when(jnp.logical_not(mine))
        def _():
            send_a[h, yy] = dq.astype(BF16)
            stage_a(h, yy).start()

        @pl.when(i == 3)
        def _():
            send_x[h] = dk_acc[...].reshape(2, 4, 128, hd).astype(BF16)
            for y in range(2):
                keep_k[lax.rem(h, 2), y] = dk_acc[pl.ds(pl.multiple_of((y * 4 + x) * 128, 128), 128), :]
            send_v[h] = dv_acc[pl.ds(pl.multiple_of((1 - yl) * rows, rows), rows), :].reshape(4, 128, hd).astype(BF16)
            keep_v[lax.rem(h, 2)] = dv_acc[pl.ds(pl.multiple_of(yl * rows, rows), rows), :].reshape(4, 128, hd)

    def step(n, carry):
        h = n // 4
        i = lax.rem(n, 4)
        for k, event in enumerate((event_0, event_1, event_2, event_3)):
            @pl.when(i == k)
            def _(event=event):
                event(h)

        @pl.when(h < heads)
        def _():
            compute(h, i)

        return carry

    lax.fori_loop(0, heads * 4 + 6, step, 0)

    def drain(h, carry):
        for slot in range(15):
            gather(h, slot).wait_send()
        for y in range(2):
            stage_a(h, y).wait_send()
        for j in range(3):
            stage_b(h, j).wait_send()
            stage_x(h, j).wait_send()
            stage_w(h, j).wait_send()
        stage_c(h).wait_send()
        stage_v(h).wait_send()
        stage_y(h).wait_send()
        return carry

    for slot in range(15):
        gather(None, slot).wait_send()
    lax.fori_loop(0, heads, drain, 0)


def finish(scale, dq_ref, dk_ref, dv_ref, q_out, k_out, v_out):
    q_out[...] = (dq_ref[...] * scale).astype(BF16)
    k_out[...] = (dk_ref[...] * scale).astype(BF16)
    v_out[...] = dv_ref[...].astype(BF16)


def shards(queries, out_grad, outputs, log_norms, src_keys, src_values, block_list, block_count, mask_bits):
    heads = log_norms.shape[0]
    local, features = queries.shape
    hd = features // heads
    n_src = src_keys.shape[0]
    tile = 128
    vmem = pl.BlockSpec(memory_space=pltpu.VMEM)
    anyspace = pl.BlockSpec(memory_space=pl.ANY)
    wide = jax.ShapeDtypeStruct((local, features), F32)
    narrow = jax.ShapeDtypeStruct((local, features), BF16)
    sums = pl.pallas_call(
        functools.partial(core, heads, tile),
        out_shape=(wide, wide, wide),
        in_specs=[pl.BlockSpec(memory_space=pltpu.SMEM), vmem] + [anyspace] * 7,
        out_specs=(vmem, vmem, vmem),
        scratch_shapes=[
            pltpu.VMEM(mask_bits.shape, jnp.int32),
            pltpu.VMEM((8, 128), jnp.int32),
            pltpu.SMEM((8, 128), jnp.int32),
            pltpu.VMEM((n_src, 16 * 128), F32),
            pltpu.VMEM((heads, 2, 2, 2, 4, 128, hd), BF16),
            pltpu.VMEM((heads, 128, hd), BF16),
            pltpu.VMEM((2, 2, 4, 2 * heads, 128), F32),
            pltpu.VMEM((heads, n_src, hd), BF16),
            pltpu.VMEM((heads, n_src, hd), BF16),
            pltpu.VMEM((hd, n_src), BF16),
            pltpu.VMEM((n_src, 512), BF16),
            pltpu.VMEM((n_src, hd), F32),
            pltpu.VMEM((n_src, hd), F32),
            pltpu.VMEM((heads, 2, 4, 128, hd), BF16),
            pltpu.VMEM((heads, 2, 4, 128, hd), BF16),
            pltpu.VMEM((2, 4, 128, hd), F32),
            pltpu.VMEM((heads, 4, 128, hd), BF16),
            pltpu.VMEM((heads, 4, 128, hd), BF16),
            pltpu.VMEM((4, 128, hd), F32),
            pltpu.VMEM((heads, 4, 128, hd), BF16),
            pltpu.VMEM((heads, 3, 128, hd), BF16),
            pltpu.VMEM((heads, 2, 4, 128, hd), BF16),
            pltpu.VMEM((heads, 3, 2, 128, hd), BF16),
            pltpu.VMEM((2, 2, 128, hd), F32),
            pltpu.VMEM((heads, 4, 128, hd), BF16),
            pltpu.VMEM((heads, 4, 128, hd), BF16),
            pltpu.VMEM((2, 4, 128, hd), F32),
            pltpu.VMEM((heads, 128, hd), BF16),
            pltpu.VMEM((heads, 128, hd), BF16),
            pltpu.VMEM((heads, 4, 128, hd), BF16),
            pltpu.VMEM((heads, 3, 128, hd), BF16),
            pltpu.SemaphoreType.DMA((heads, 5)),
            pltpu.SemaphoreType.DMA((3,)),
            pltpu.SemaphoreType.DMA((heads, 15)),
            pltpu.SemaphoreType.DMA((heads, 15)),
            pltpu.SemaphoreType.DMA((15,)),
            pltpu.SemaphoreType.DMA((15,)),
            pltpu.SemaphoreType.DMA((heads, 14)),
            pltpu.SemaphoreType.DMA((heads, 14)),
        ],
        compiler_params=pltpu.CompilerParams(
            vmem_limit_bytes=48 << 20, collective_id=0, has_side_effects=True
        ),
        name="attention",
    )(block_count, block_list, mask_bits, queries, out_grad, outputs, log_norms, src_keys, src_values)
    return pl.pallas_call(
        functools.partial(finish, hd ** -0.5),
        out_shape=(narrow, narrow, narrow),
        in_specs=[vmem] * 3,
        out_specs=(vmem, vmem, vmem),
        name="finish",
    )(*sums)


def solution(mesh):
    rows = P(("src", "rep"), None)
    placed = (
        rows,
        rows,
        rows,
        P(None, ("src", "rep")),
        P("src", None),
        P("src", None),
        P("src", "rep", None, None),
        P("src", "rep"),
        P("src", "rep", None, None, None),
    )
    return jax.shard_map(shards, mesh=mesh, in_specs=placed, out_specs=(rows, rows, rows), check_vma=False)
```

```python
import functools
import math

import jax
import jax.numpy as jnp
from jax import lax
from jax.experimental import pallas as pl
from jax.experimental.pallas import tpu as pltpu
from jax.sharding import PartitionSpec as P

F32 = jnp.float32
BF16 = jnp.bfloat16
LOG2E = math.log2(math.e)
MESH = pl.DeviceIdType.MESH


def nt_dot(a, b):
    return lax.dot_general(a, b, (((1,), (1,)), ((), ())), preferred_element_type=F32)


def nn_dot(a, b):
    return lax.dot_general(a, b, (((1,), (0,)), ((), ())), preferred_element_type=F32)


def tn_dot(a, b):
    return lax.dot_general(a, b, (((0,), (0,)), ((), ())), preferred_element_type=F32)


def build_masks(u, dest, src_blocks, table, words_ref, mask_ref):
    row = lax.broadcasted_iota(jnp.int32, (16, 128), 0)
    lane = lax.broadcasted_iota(jnp.int32, (16, 128), 1)
    half = jnp.where(lax.rem(lane, 16) >= 8, 8, 0)
    spread = jnp.where(row == lane // 16 + half, 1.0, 0.0).astype(BF16)
    bit = jnp.left_shift(1, lax.rem(lax.broadcasted_iota(jnp.int32, (1, 128), 1), 8))
    words = jnp.concatenate(
        [
            words_ref[0, 0, jnp.clip(table[0, dest * src_blocks + j], 0, words_ref.shape[2] - 1)] * table[1, dest * src_blocks + j]
            for j in range(src_blocks)
        ],
        axis=1,
    )
    halves = jnp.concatenate(
        [jnp.bitwise_and(words, 255), jnp.bitwise_and(jnp.right_shift(words, 8), 255)], axis=0
    )
    wide = tn_dot(halves.astype(F32).astype(BF16), spread).astype(jnp.int32)
    picked = jnp.where(jnp.bitwise_and(wide, bit) != 0, 1.0, 0.0)
    mask_ref[:, pl.ds(pl.multiple_of(u * 128, 128), 128)] = picked


def visit(scale, tile, q, g, norm, delta, k_ref, v_ref, kt, mask_ref, at, dk_ref, dv_ref, sbuf):
    n_src = k_ref.shape[0]
    rows = q.shape[0]
    for c in range(n_src // tile):
        cs = pl.ds(c * tile, tile)
        s = nt_dot(k_ref[cs, :], q)
        e = jnp.exp2(s * (scale * LOG2E) - norm)
        p = e * mask_ref[cs, pl.ds(at, rows)]
        d = nt_dot(v_ref[cs, :], g)
        ds = p * (d - delta)
        p_low = p.astype(BF16)
        s_low = ds.astype(BF16)
        sbuf[cs, :] = s_low
        dv_ref[cs, :] += nn_dot(p_low, g)
        dk_ref[cs, :] += nn_dot(s_low, q)
    return nn_dot(kt, sbuf[...])


def pair_slots(list_ref, count, src_blocks, n_pairs):
    capacity = list_ref.shape[3]
    code = list_ref[0, 0, 0:1, :] * src_blocks + list_ref[0, 0, 1:2, :]
    order = lax.broadcasted_iota(jnp.int32, (n_pairs, capacity), 1)
    pair = lax.broadcasted_iota(jnp.int32, (n_pairs, capacity), 0)
    hit = (code == pair) & (order < count)
    slot = jnp.sum(jnp.where(hit, order, 0), axis=1, keepdims=True)
    live = jnp.sum(jnp.where(hit, 1, 0), axis=1, keepdims=True)
    column = lax.broadcasted_iota(jnp.int32, (n_pairs, 128), 1)
    both = jnp.where(column == 0, slot, jnp.where(column == 1, live, 0))
    return both.T[0:8]


def core(heads, tile, count_ref, list_ref, words_hbm, q_hbm, g_hbm, o_hbm, norm_hbm, k_hbm, v_hbm,
         dq_ref, dk_ref, dv_ref,
         words, slots, table, mask_ref, qg, o_all, nd, k_all, v_all, kt, sbuf, dk_acc, dv_acc,
         send_a, recv_a, acc_a, send_c, recv_c, tot_b, send_b, recv_b,
         send_x, recv_x, keep_k, send_v, recv_v, keep_v, send_y, recv_y, send_w, recv_w,
         local_sem, extra_sem, ag_send, ag_recv, nd_send, nd_recv, rs_send, rs_recv):
    hd = kt.shape[0]
    n_src = kt.shape[1]
    src_blocks = n_src // 128
    rows = 4 * 128
    scale = hd ** -0.5
    src, rep = lax.axis_index("src"), lax.axis_index("rep")
    yh, z, c = src // 8, lax.rem(src, 8) // 2, lax.rem(src, 2)
    yl, x = rep // 4, lax.rem(rep, 4)

    def at_src(yy, zz, cc):
        return {"src": yy * 8 + zz * 2 + cc, "rep": rep}

    def at_rep(yy, xx):
        return {"src": src, "rep": yy * 4 + xx}

    sibling = at_src(yh, z, 1 - c)
    across = at_src(1 - yh, z, c)
    zs = [lax.rem(z + d, 4) for d in (1, 2, 3)]
    xs = [lax.rem(x + d, 4) for d in (1, 2, 3)]
    around = [at_src(yh, zz, c) for zz in zs]
    beside = [at_rep(yl, xx) for xx in xs]
    over = at_rep(1 - yl, x)

    barrier = pltpu.get_barrier_semaphore()
    for peer in [sibling, across, over] + around + beside:
        pl.semaphore_signal(barrier, inc=1, device_id=peer, device_id_type=MESH)

    mine_copies, kv_copies = [], []
    for h in range(heads):
        cols = pl.ds(h * hd, hd)
        for i, (a, b) in enumerate((
            (q_hbm, qg.at[h, c, yh, 0, z]), (g_hbm, qg.at[h, c, yh, 1, z]), (o_hbm, o_all.at[h]),
            (k_hbm, k_all.at[h]), (v_hbm, v_all.at[h]),
        )):
            cp = pltpu.make_async_copy(a.at[:, cols], b, local_sem.at[h, i])
            if i < 3:
                cp.start()
                mine_copies.append(cp)
            else:
                kv_copies.append(cp)
    norm_copy = pltpu.make_async_copy(norm_hbm, nd.at[c, yh, z, pl.ds(0, heads)], extra_sem.at[0])
    norm_copy.start()
    words_copy = pltpu.make_async_copy(words_hbm, words, extra_sem.at[1])
    words_copy.start()
    for cp in kv_copies:
        cp.start()

    slots[...] = pair_slots(list_ref, count_ref[0, 0], src_blocks, 128)
    table_copy = pltpu.make_async_copy(slots, table, extra_sem.at[2])
    table_copy.start()

    norm_copy.wait()
    for cp in mine_copies:
        cp.wait()
    for h in range(heads):
        product = qg[h, c, yh, 1, z].astype(F32) * o_all[h].astype(F32)
        nd[c, yh, z, heads + h : heads + h + 1, :] = jnp.sum(product.T, axis=0, keepdims=True)

    def remote(a, b, s, r, peer):
        return pltpu.make_async_remote_copy(
            src_ref=a, dst_ref=b, send_sem=s, recv_sem=r, device_id=peer, device_id_type=MESH
        )

    def gather_copy(h, cc, yy, zz, slot, peer):
        if h is None:
            ref = nd.at[cc, yy, zz]
            return remote(ref, ref, nd_send.at[slot], nd_recv.at[slot], peer)
        ref = qg.at[h, cc, yy, :, zz]
        return remote(ref, ref, ag_send.at[h, slot], ag_recv.at[h, slot], peer)

    def gather(h, slot):
        if slot == 0:
            yy, zz, peer = yh, z, across
        elif slot < 4:
            yy, zz, peer = yh, z, around[slot - 1]
        elif slot < 7:
            yy, zz, peer = 1 - yh, z, around[slot - 4]
        elif slot == 7:
            yy, zz, peer = yh, z, sibling
        elif slot == 8:
            yy, zz, peer = 1 - yh, z, sibling
        elif slot < 12:
            yy, zz, peer = yh, zs[slot - 9], sibling
        else:
            yy, zz, peer = 1 - yh, zs[slot - 12], sibling
        return gather_copy(h, c, yy, zz, slot, peer)

    def arrived(h, slot):
        if slot == 0:
            cc, yy, zz = c, 1 - yh, z
        elif slot < 4:
            cc, yy, zz = c, yh, zs[3 - slot]
        elif slot < 7:
            cc, yy, zz = c, 1 - yh, zs[6 - slot]
        elif slot == 7:
            cc, yy, zz = 1 - c, yh, z
        elif slot == 8:
            cc, yy, zz = 1 - c, 1 - yh, z
        elif slot < 12:
            cc, yy, zz = 1 - c, yh, zs[slot - 9]
        else:
            cc, yy, zz = 1 - c, 1 - yh, zs[slot - 12]
        gather_copy(h, cc, yy, zz, slot, sibling).wait_recv()

    def send_own(h):
        for slot in (1, 3, 2, 7):
            gather(h, slot).start()

    def relay_across(h):
        arrived(h, 0)
        for slot in (4, 6, 5, 8):
            gather(h, slot).start()

    def forward_own_row(h):
        for d in (1, 3, 2):
            arrived(h, d)
            gather(h, 12 - d).start()

    def forward_other_row(h):
        for d in (1, 3, 2):
            arrived(h, 3 + d)
            gather(h, 15 - d).start()

    def sibling_own_row(h):
        for slot in (7, 9, 10, 11):
            arrived(h, slot)

    def sibling_other_row(h):
        for slot in (8, 12, 13, 14):
            arrived(h, slot)

    def stage_a(h, y):
        return remote(send_a.at[h, y], recv_a.at[h, y], rs_send.at[h, y], rs_recv.at[h, y], sibling)

    def stage_c(h):
        return remote(send_c.at[h], recv_c.at[h], rs_send.at[h, 2], rs_recv.at[h, 2], across)

    def stage_b(h, j):
        return remote(send_b.at[h, zs[j]], recv_b.at[h, j], rs_send.at[h, 3 + j], rs_recv.at[h, 3 + j], around[j])

    def stage_x(h, j):
        return remote(send_x.at[h, :, xs[j]], recv_x.at[h, j], rs_send.at[h, 6 + j], rs_recv.at[h, 6 + j], beside[j])

    def stage_v(h):
        return remote(send_v.at[h], recv_v.at[h], rs_send.at[h, 9], rs_recv.at[h, 9], over)

    def stage_y(h):
        return remote(send_y.at[h], recv_y.at[h], rs_send.at[h, 10], rs_recv.at[h, 10], over)

    def stage_w(h, j):
        return remote(send_w.at[h, xs[j]], recv_w.at[h, j], rs_send.at[h, 11 + j], rs_recv.at[h, 11 + j], beside[j])

    def masks(cc, yy):
        for zz in range(4):
            build_masks((cc * 2 + yy) * 4 + zz, yy * 8 + zz * 2 + cc, src_blocks, table, words, mask_ref)

    pl.semaphore_wait(barrier, 9)
    send_own(0)
    gather(0, 0).start()
    send_own(None)
    gather(None, 0).start()
    for h in range(1, heads):
        gather(h, 0).start()
    words_copy.wait()
    table_copy.wait()
    masks(c, yh)
    relay_across(0)
    relay_across(None)
    masks(1 - c, yh)
    forward_own_row(0)
    forward_own_row(None)

    def exchange_rows(h):
        stage_a(h, 1 - yh).wait_recv()
        send_c[h] = (acc_a[1 - yh] + recv_a[h, 1 - yh].astype(F32)).astype(BF16)
        stage_c(h).start()

    def event_0(h):
        done = h - 1

        @pl.when((h >= 1) & (h <= heads))
        def _():
            for j in (0, 2, 1):
                stage_x(done, j).start()
            stage_v(done).start()

        @pl.when(h == 1)
        def _():
            exchange_rows(0)

        @pl.when(h + 1 < heads)
        def _():
            send_own(h + 1)
            relay_across(h + 1)

        @pl.when((h >= 1) & (h < heads))
        def _():
            forward_other_row(h)
            sibling_own_row(h)

    def event_1(h):
        @pl.when(h >= 2)
        def _():
            cols = pl.ds(pl.multiple_of((h - 2) * hd, hd), hd)
            for j in range(3):
                stage_b((h - 2), j).wait_recv()
            dq_ref[:, cols] = (
                tot_b[z]
                + recv_b[(h - 2), 0].astype(F32)
                + recv_b[(h - 2), 1].astype(F32)
                + recv_b[(h - 2), 2].astype(F32)
            )

        @pl.when(h == 0)
        def _():
            sibling_own_row(None)
            sibling_own_row(0)

        @pl.when((h >= 1) & (h < heads))
        def _():
            sibling_other_row(h)

    def event_2(h):
        done = h - 1

        @pl.when((h >= 1) & (h <= heads))
        def _():
            stage_a(done, yh).wait_recv()
            stage_c(done).wait_recv()
            total = acc_a[yh] + recv_a[done, yh].astype(F32) + recv_c[done].astype(F32)
            tot_b[...] = total
            send_b[done] = total.astype(BF16)
            for j in (0, 2, 1):
                stage_b(done, j).start()

        @pl.when(h >= 2)
        def _():
            cols = pl.ds(pl.multiple_of((h - 2) * hd, hd), hd)
            stage_y(h - 2).wait_recv()
            dk_ref[:, cols] = keep_k[lax.rem(h, 2), yl] + recv_y[h - 2].astype(F32)
            for j in range(3):
                stage_w(h - 2, j).wait_recv()
            dv_ref[:, cols] = (
                keep_v[lax.rem(h, 2), x]
                + recv_w[h - 2, 0].astype(F32)
                + recv_w[h - 2, 1].astype(F32)
                + recv_w[h - 2, 2].astype(F32)
            )

        @pl.when(h == 0)
        def _():
            forward_other_row(None)
            forward_other_row(0)
            masks(c, 1 - yh)

        @pl.when(h + 1 < heads)
        def _():
            forward_own_row(h + 1)

    def event_3(h):
        done = h - 1

        odd = lax.rem(h + 1, 2)

        @pl.when((h >= 1) & (h <= heads))
        def _():
            for j in range(3):
                stage_x(done, j).wait_recv()
            for y in range(2):
                keep_k[odd, y] = (
                    keep_k[odd, y]
                    + recv_x[done, 0, y].astype(F32)
                    + recv_x[done, 1, y].astype(F32)
                    + recv_x[done, 2, y].astype(F32)
                )
            send_y[done] = keep_k[odd, 1 - yl].astype(BF16)
            stage_y(done).start()
            stage_v(done).wait_recv()
            total = keep_v[odd] + recv_v[done].astype(F32)
            keep_v[odd] = total
            send_w[done] = total.astype(BF16)
            for j in (0, 2, 1):
                stage_w(done, j).start()

        @pl.when(h == 0)
        def _():
            sibling_other_row(None)
            sibling_other_row(0)
            masks(1 - c, 1 - yh)

        @pl.when((h >= 1) & (h < heads))
        def _():
            exchange_rows(h)

    def compute(h, i):
        @pl.when((h == 0) & (i == 0))
        def _():
            for cp in kv_copies:
                cp.wait()

        @pl.when(i == 0)
        def _():
            kt[...] = k_all[h].T
            dk_acc[...] = jnp.zeros_like(dk_acc)
            dv_acc[...] = jnp.zeros_like(dv_acc)

        mine = jnp.where(h == 0, lax.rem(i, 2) == 0, i >= 2)
        own_row = jnp.where(h == 0, i < 2, (i == 0) | (i == 3))
        cc = jnp.where(mine, c, 1 - c)
        yy = jnp.where(own_row, yh, 1 - yh)
        at = pl.multiple_of((cc * 2 + yy) * rows, rows)
        q = qg[h, cc, yy, 0].reshape(rows, hd)
        g = qg[h, cc, yy, 1].reshape(rows, hd)
        norm = jnp.concatenate([nd[cc, yy, j, pl.ds(h, 1), :] for j in range(4)], axis=1) * LOG2E
        delta = jnp.concatenate([nd[cc, yy, j, pl.ds(heads + h, 1), :] for j in range(4)], axis=1)
        dqt = visit(scale, tile, q, g, norm, delta, k_all.at[h], v_all.at[h], kt[...], mask_ref, at,
                    dk_acc, dv_acc, sbuf)
        dq = dqt.T.reshape(4, 128, hd)

        @pl.when(mine)
        def _():
            acc_a[yy] = dq

        @pl.when(jnp.logical_not(mine))
        def _():
            send_a[h, yy] = dq.astype(BF16)
            stage_a(h, yy).start()

        @pl.when(i == 3)
        def _():
            send_x[h] = dk_acc[...].reshape(2, 4, 128, hd).astype(BF16)
            for y in range(2):
                keep_k[lax.rem(h, 2), y] = dk_acc[pl.ds(pl.multiple_of((y * 4 + x) * 128, 128), 128), :]
            send_v[h] = dv_acc[pl.ds(pl.multiple_of((1 - yl) * rows, rows), rows), :].reshape(4, 128, hd).astype(BF16)
            keep_v[lax.rem(h, 2)] = dv_acc[pl.ds(pl.multiple_of(yl * rows, rows), rows), :].reshape(4, 128, hd)

    def step(n, carry):
        h = n // 4
        i = lax.rem(n, 4)
        for k, event in enumerate((event_0, event_1, event_2, event_3)):
            @pl.when(i == k)
            def _(event=event):
                event(h)

        @pl.when(h < heads)
        def _():
            compute(h, i)

        return carry

    lax.fori_loop(0, heads * 4 + 7, step, 0)

    def drain(h, carry):
        for slot in range(15):
            gather(h, slot).wait_send()
        for y in range(2):
            stage_a(h, y).wait_send()
        for j in range(3):
            stage_b(h, j).wait_send()
            stage_x(h, j).wait_send()
            stage_w(h, j).wait_send()
        stage_c(h).wait_send()
        stage_v(h).wait_send()
        stage_y(h).wait_send()
        return carry

    for slot in range(15):
        gather(None, slot).wait_send()
    lax.fori_loop(0, heads, drain, 0)


def finish(scale, dq_ref, dk_ref, dv_ref, q_out, k_out, v_out):
    q_out[...] = (dq_ref[...] * scale).astype(BF16)
    k_out[...] = (dk_ref[...] * scale).astype(BF16)
    v_out[...] = dv_ref[...].astype(BF16)


def shards(queries, out_grad, outputs, log_norms, src_keys, src_values, block_list, block_count, mask_bits):
    heads = log_norms.shape[0]
    local, features = queries.shape
    hd = features // heads
    n_src = src_keys.shape[0]
    tile = 256
    vmem = pl.BlockSpec(memory_space=pltpu.VMEM)
    anyspace = pl.BlockSpec(memory_space=pl.ANY)
    wide = jax.ShapeDtypeStruct((local, features), F32)
    narrow = jax.ShapeDtypeStruct((local, features), BF16)
    sums = pl.pallas_call(
        functools.partial(core, heads, tile),
        out_shape=(wide, wide, wide),
        in_specs=[pl.BlockSpec(memory_space=pltpu.SMEM), vmem] + [anyspace] * 7,
        out_specs=(vmem, vmem, vmem),
        scratch_shapes=[
            pltpu.VMEM(mask_bits.shape, jnp.int32),
            pltpu.VMEM((8, 128), jnp.int32),
            pltpu.SMEM((8, 128), jnp.int32),
            pltpu.VMEM((n_src, 16 * 128), F32),
            pltpu.VMEM((heads, 2, 2, 2, 4, 128, hd), BF16),
            pltpu.VMEM((heads, 128, hd), BF16),
            pltpu.VMEM((2, 2, 4, 2 * heads, 128), F32),
            pltpu.VMEM((heads, n_src, hd), BF16),
            pltpu.VMEM((heads, n_src, hd), BF16),
            pltpu.VMEM((hd, n_src), BF16),
            pltpu.VMEM((n_src, 512), BF16),
            pltpu.VMEM((n_src, hd), F32),
            pltpu.VMEM((n_src, hd), F32),
            pltpu.VMEM((heads, 2, 4, 128, hd), BF16),
            pltpu.VMEM((heads, 2, 4, 128, hd), BF16),
            pltpu.VMEM((2, 4, 128, hd), F32),
            pltpu.VMEM((heads, 4, 128, hd), BF16),
            pltpu.VMEM((heads, 4, 128, hd), BF16),
            pltpu.VMEM((4, 128, hd), F32),
            pltpu.VMEM((heads, 4, 128, hd), BF16),
            pltpu.VMEM((heads, 3, 128, hd), BF16),
            pltpu.VMEM((heads, 2, 4, 128, hd), BF16),
            pltpu.VMEM((heads, 3, 2, 128, hd), BF16),
            pltpu.VMEM((2, 2, 128, hd), F32),
            pltpu.VMEM((heads, 4, 128, hd), BF16),
            pltpu.VMEM((heads, 4, 128, hd), BF16),
            pltpu.VMEM((2, 4, 128, hd), F32),
            pltpu.VMEM((heads, 128, hd), BF16),
            pltpu.VMEM((heads, 128, hd), BF16),
            pltpu.VMEM((heads, 4, 128, hd), BF16),
            pltpu.VMEM((heads, 3, 128, hd), BF16),
            pltpu.SemaphoreType.DMA((heads, 5)),
            pltpu.SemaphoreType.DMA((3,)),
            pltpu.SemaphoreType.DMA((heads, 15)),
            pltpu.SemaphoreType.DMA((heads, 15)),
            pltpu.SemaphoreType.DMA((15,)),
            pltpu.SemaphoreType.DMA((15,)),
            pltpu.SemaphoreType.DMA((heads, 14)),
            pltpu.SemaphoreType.DMA((heads, 14)),
        ],
        compiler_params=pltpu.CompilerParams(
            vmem_limit_bytes=67043328, collective_id=0, has_side_effects=True
        ),
        name="attention",
    )(block_count, block_list, mask_bits, queries, out_grad, outputs, log_norms, src_keys, src_values)
    return pl.pallas_call(
        functools.partial(finish, hd ** -0.5),
        out_shape=(narrow, narrow, narrow),
        in_specs=[vmem] * 3,
        out_specs=(vmem, vmem, vmem),
        name="finish",
    )(*sums)


def solution(mesh):
    rows = P(("src", "rep"), None)
    placed = (
        rows,
        rows,
        rows,
        P(None, ("src", "rep")),
        P("src", None),
        P("src", None),
        P("src", "rep", None, None),
        P("src", "rep"),
        P("src", "rep", None, None, None),
    )
    return jax.shard_map(shards, mesh=mesh, in_specs=placed, out_specs=(rows, rows, rows), check_vma=False)
```

```python
import functools
import math

import jax
import jax.numpy as jnp
from jax import lax
from jax.experimental import pallas as pl
from jax.experimental.pallas import tpu as pltpu
from jax.sharding import PartitionSpec as P

F32 = jnp.float32
BF16 = jnp.bfloat16
LOG2E = math.log2(math.e)
MESH = pl.DeviceIdType.MESH


def nt_dot(a, b):
    return lax.dot_general(a, b, (((1,), (1,)), ((), ())), preferred_element_type=F32)


def nn_dot(a, b):
    return lax.dot_general(a, b, (((1,), (0,)), ((), ())), preferred_element_type=F32)


def tn_dot(a, b):
    return lax.dot_general(a, b, (((0,), (0,)), ((), ())), preferred_element_type=F32)


def build_masks(u, dest, src_blocks, table, words_ref, mask_ref):
    row = lax.broadcasted_iota(jnp.int32, (16, 128), 0)
    lane = lax.broadcasted_iota(jnp.int32, (16, 128), 1)
    half = jnp.where(lax.rem(lane, 16) >= 8, 8, 0)
    spread = jnp.where(row == lane // 16 + half, 1.0, 0.0).astype(BF16)
    bit = jnp.left_shift(1, lax.rem(lax.broadcasted_iota(jnp.int32, (1, 128), 1), 8))
    words = jnp.concatenate(
        [
            words_ref[0, 0, jnp.clip(table[0, dest * src_blocks + j], 0, words_ref.shape[2] - 1)] * table[1, dest * src_blocks + j]
            for j in range(src_blocks)
        ],
        axis=1,
    )
    halves = jnp.concatenate(
        [jnp.bitwise_and(words, 255), jnp.bitwise_and(jnp.right_shift(words, 8), 255)], axis=0
    )
    wide = tn_dot(halves.astype(F32).astype(BF16), spread).astype(jnp.int32)
    picked = jnp.where(jnp.bitwise_and(wide, bit) != 0, 1.0, 0.0)
    mask_ref[:, pl.ds(pl.multiple_of(u * 128, 128), 128)] = picked


def visit(scale, tile, q, g, norm, delta, k_ref, v_ref, kt, mask_ref, at, dk_ref, dv_ref, sbuf):
    n_src = k_ref.shape[0]
    rows = q.shape[0]
    for c in range(n_src // tile):
        cs = pl.ds(c * tile, tile)
        s = nt_dot(k_ref[cs, :], q)
        e = jnp.exp2(s * (scale * LOG2E) - norm)
        p = e * mask_ref[cs, pl.ds(at, rows)]
        d = nt_dot(v_ref[cs, :], g)
        ds = p * (d - delta)
        p_low = p.astype(BF16)
        s_low = ds.astype(BF16)
        sbuf[cs, :] = s_low
        dv_ref[cs, :] += nn_dot(p_low, g)
        dk_ref[cs, :] += nn_dot(s_low, q)
    return nn_dot(kt, sbuf[...])


def pair_slots(list_ref, count, src_blocks, n_pairs):
    capacity = list_ref.shape[3]
    code = list_ref[0, 0, 0:1, :] * src_blocks + list_ref[0, 0, 1:2, :]
    order = lax.broadcasted_iota(jnp.int32, (n_pairs, capacity), 1)
    pair = lax.broadcasted_iota(jnp.int32, (n_pairs, capacity), 0)
    hit = (code == pair) & (order < count)
    slot = jnp.sum(jnp.where(hit, order, 0), axis=1, keepdims=True)
    live = jnp.sum(jnp.where(hit, 1, 0), axis=1, keepdims=True)
    column = lax.broadcasted_iota(jnp.int32, (n_pairs, 128), 1)
    both = jnp.where(column == 0, slot, jnp.where(column == 1, live, 0))
    return both.T[0:8]


def core(heads, tile, count_ref, list_ref, words_hbm, q_hbm, g_hbm, o_hbm, norm_hbm, k_hbm, v_hbm,
         dq_ref, dk_ref, dv_ref,
         words, slots, table, mask_ref, qg, o_all, nd, k_all, v_all, kt, sbuf, dk_acc, dv_acc,
         send_a, recv_a, acc_a, send_c, recv_c, tot_b, send_b, recv_b,
         send_x, recv_x, keep, send_y, recv_y, recv_v, tot_w, send_w, recv_w,
         local_sem, extra_sem, ag_send, ag_recv, nd_send, nd_recv, rs_send, rs_recv):
    hd = kt.shape[0]
    n_src = kt.shape[1]
    src_blocks = n_src // 128
    rows = 4 * 128
    scale = hd ** -0.5
    src, rep = lax.axis_index("src"), lax.axis_index("rep")
    yh, z, c = src // 8, lax.rem(src, 8) // 2, lax.rem(src, 2)
    yl, x = rep // 4, lax.rem(rep, 4)

    def at_src(yy, zz, cc):
        return {"src": yy * 8 + zz * 2 + cc, "rep": rep}

    def at_rep(yy, xx):
        return {"src": src, "rep": yy * 4 + xx}

    sibling = at_src(yh, z, 1 - c)
    across = at_src(1 - yh, z, c)
    zs = [lax.rem(z + d, 4) for d in (1, 2, 3)]
    xs = [lax.rem(x + d, 4) for d in (1, 2, 3)]
    around = [at_src(yh, zz, c) for zz in zs]
    beside = [at_rep(yl, xx) for xx in xs]
    over = at_rep(1 - yl, x)

    barrier = pltpu.get_barrier_semaphore()
    for peer in [sibling, across, over] + around + beside:
        pl.semaphore_signal(barrier, inc=1, device_id=peer, device_id_type=MESH)

    mine_copies, kv_copies = [], []
    for h in range(heads):
        cols = pl.ds(h * hd, hd)
        for i, (a, b) in enumerate((
            (q_hbm, qg.at[h, c, yh, 0, z]), (g_hbm, qg.at[h, c, yh, 1, z]), (o_hbm, o_all.at[h]),
            (k_hbm, k_all.at[h]), (v_hbm, v_all.at[h]),
        )):
            cp = pltpu.make_async_copy(a.at[:, cols], b, local_sem.at[h, i])
            if i < 3:
                cp.start()
                mine_copies.append(cp)
            else:
                kv_copies.append(cp)
    norm_copy = pltpu.make_async_copy(norm_hbm, nd.at[c, yh, z, pl.ds(0, heads)], extra_sem.at[0])
    norm_copy.start()
    words_copy = pltpu.make_async_copy(words_hbm, words, extra_sem.at[1])
    words_copy.start()
    for cp in kv_copies:
        cp.start()

    slots[...] = pair_slots(list_ref, count_ref[0, 0], src_blocks, 128)
    table_copy = pltpu.make_async_copy(slots, table, extra_sem.at[2])
    table_copy.start()

    def remote(a, b, s, r, peer):
        return pltpu.make_async_remote_copy(
            src_ref=a, dst_ref=b, send_sem=s, recv_sem=r, device_id=peer, device_id_type=MESH
        )

    def gather_copy(h, cc, yy, zz, slot, peer):
        if h is None:
            ref = nd.at[cc, yy, zz]
            return remote(ref, ref, nd_send.at[slot], nd_recv.at[slot], peer)
        ref = qg.at[h, cc, yy, :, zz]
        return remote(ref, ref, ag_send.at[h, slot], ag_recv.at[h, slot], peer)

    def gather(h, slot):
        if slot == 0:
            yy, zz, peer = yh, z, across
        elif slot < 4:
            yy, zz, peer = yh, z, around[slot - 1]
        elif slot < 7:
            yy, zz, peer = 1 - yh, z, around[slot - 4]
        elif slot == 7:
            yy, zz, peer = yh, z, sibling
        elif slot == 8:
            yy, zz, peer = 1 - yh, z, sibling
        elif slot < 12:
            yy, zz, peer = yh, zs[slot - 9], sibling
        else:
            yy, zz, peer = 1 - yh, zs[slot - 12], sibling
        return gather_copy(h, c, yy, zz, slot, peer)

    def arrived(h, slot):
        if slot == 0:
            cc, yy, zz = c, 1 - yh, z
        elif slot < 4:
            cc, yy, zz = c, yh, zs[3 - slot]
        elif slot < 7:
            cc, yy, zz = c, 1 - yh, zs[6 - slot]
        elif slot == 7:
            cc, yy, zz = 1 - c, yh, z
        elif slot == 8:
            cc, yy, zz = 1 - c, 1 - yh, z
        elif slot < 12:
            cc, yy, zz = 1 - c, yh, zs[slot - 9]
        else:
            cc, yy, zz = 1 - c, 1 - yh, zs[slot - 12]
        gather_copy(h, cc, yy, zz, slot, sibling).wait_recv()

    def send_own(h):
        for slot in (1, 3, 2, 7):
            gather(h, slot).start()

    def relay_across(h):
        arrived(h, 0)
        for slot in (4, 6, 5, 8):
            gather(h, slot).start()

    def forward_own_row(h):
        for d in (1, 3, 2):
            arrived(h, d)
            gather(h, 12 - d).start()

    def forward_other_row(h):
        for d in (1, 3, 2):
            arrived(h, 3 + d)
            gather(h, 15 - d).start()

    def half(h, yy, zz, part, slot, peer):
        ref = qg.at[h, c, yy, part, zz]
        return remote(ref, ref, ag_send.at[h, slot], ag_recv.at[h, slot], peer)

    def ring_own(h):
        for slot in (1, 3, 7):
            gather(h, slot).start()

    def ring_across(h):
        arrived(h, 0)
        for slot in (4, 6, 8):
            gather(h, slot).start()

    def ring_halves(h):
        return [
            (1, 11, half(h, yh, zs[2], 0, 2, around[0])),
            (3, 9, half(h, yh, zs[0], 1, 15, around[2])),
            (4, 14, half(h, 1 - yh, zs[2], 0, 5, around[0])),
            (6, 12, half(h, 1 - yh, zs[0], 1, 16, around[2])),
        ]

    def ring_forward(h):
        for slot, core_slot, onward in ring_halves(h):
            arrived(h, slot)
            onward.start()
            gather(h, core_slot).start()

    def ring_finish(h):
        for yy, slots_, core_slot in ((yh, (2, 15), 10), (1 - yh, (5, 16), 13)):
            for part in range(2):
                half(h, yy, zs[1], part, slots_[part], sibling).wait_recv()
            gather(h, core_slot).start()

    def sibling_own_row(h):
        for slot in (7, 9, 10, 11):
            arrived(h, slot)

    def sibling_other_row(h):
        for slot in (8, 12, 13, 14):
            arrived(h, slot)

    def stage_a(h, y):
        return remote(send_a.at[h, y], recv_a.at[h, y], rs_send.at[h, y], rs_recv.at[h, y], sibling)

    def stage_c(h):
        return remote(send_c.at[h], recv_c.at[h], rs_send.at[h, 2], rs_recv.at[h, 2], across)

    def stage_b(h, j):
        return remote(send_b.at[h, zs[j]], recv_b.at[h, j], rs_send.at[h, 3 + j], rs_recv.at[h, 3 + j], around[j])

    def stage_x(h, j):
        return remote(send_x.at[h, :, :, xs[j]], recv_x.at[h, j], rs_send.at[h, 6 + j], rs_recv.at[h, 6 + j], beside[j])

    def stage_y(h):
        return remote(send_y.at[h], recv_y.at[h], rs_send.at[h, 9], rs_recv.at[h, 9], over)

    last = heads - 1

    def last_x(j):
        return remote(send_x.at[last, 0, :, xs[j]], recv_x.at[last, j, 0], rs_send.at[last, 6 + j],
                      rs_recv.at[last, 6 + j], beside[j])

    def last_y():
        return remote(send_y.at[last, 0], recv_y.at[last, 0], rs_send.at[last, 9], rs_recv.at[last, 9], over)

    def last_v():
        return remote(send_x.at[last, 1, 1 - yl], recv_v, rs_send.at[last, 10], rs_recv.at[last, 10], over)

    def last_w(j):
        return remote(send_w.at[xs[j]], recv_w.at[j], rs_send.at[last, 11 + j], rs_recv.at[last, 11 + j], beside[j])

    def masks(cc, yy):
        for zz in range(4):
            build_masks((cc * 2 + yy) * 4 + zz, yy * 8 + zz * 2 + cc, src_blocks, table, words, mask_ref)

    for cp in mine_copies[:2]:
        cp.wait()
    pl.semaphore_wait(barrier, 9)
    send_own(0)
    gather(0, 0).start()
    norm_copy.wait()
    for cp in mine_copies[2:]:
        cp.wait()
    for h in range(heads):
        product = qg[h, c, yh, 1, z].astype(F32) * o_all[h].astype(F32)
        nd[c, yh, z, heads + h : heads + h + 1, :] = jnp.sum(product.T, axis=0, keepdims=True)
    send_own(None)
    gather(None, 0).start()
    for h in range(1, heads):
        gather(h, 0).start()
    words_copy.wait()
    table_copy.wait()
    masks(c, yh)
    relay_across(0)
    relay_across(None)
    masks(1 - c, yh)
    forward_own_row(0)
    forward_own_row(None)

    def exchange_rows(h):
        stage_a(h, 1 - yh).wait_recv()
        send_c[h] = (acc_a[1 - yh] + recv_a[h, 1 - yh].astype(F32)).astype(BF16)
        stage_c(h).start()

    def event_0(h):
        done = h - 1

        @pl.when((h >= 1) & (h < heads))
        def _():
            for j in (0, 2, 1):
                stage_x(done, j).start()

        @pl.when(h == heads)
        def _():
            last_v().start()
            for j in (0, 2, 1):
                last_x(j).start()

        @pl.when(h == 1)
        def _():
            exchange_rows(0)

        @pl.when(h == 0)
        def _():
            send_own(1)
            relay_across(1)

        @pl.when(h == 1)
        def _():
            forward_other_row(1)

        @pl.when((h >= 1) & (h < heads))
        def _():
            sibling_own_row(h)

        @pl.when((h >= 2) & (h <= heads))
        def _():
            for j in range(3):
                stage_x(h - 2, j).wait_recv()
            for a in range(2):
                for y in range(2):
                    keep[lax.rem(h, 2), a, y] = (
                        keep[lax.rem(h, 2), a, y]
                        + recv_x[h - 2, 0, a, y].astype(F32)
                        + recv_x[h - 2, 1, a, y].astype(F32)
                        + recv_x[h - 2, 2, a, y].astype(F32)
                    )
                send_y[h - 2, a] = keep[lax.rem(h, 2), a, 1 - yl].astype(BF16)
            stage_y(h - 2).start()

    def event_1(h):
        @pl.when(h >= 2)
        def _():
            cols = pl.ds(pl.multiple_of((h - 2) * hd, hd), hd)
            for j in range(3):
                stage_b((h - 2), j).wait_recv()
            dq_ref[:, cols] = (
                tot_b[z]
                + recv_b[(h - 2), 0].astype(F32)
                + recv_b[(h - 2), 1].astype(F32)
                + recv_b[(h - 2), 2].astype(F32)
            )

        @pl.when(h == 0)
        def _():
            sibling_own_row(None)
            sibling_own_row(0)

        @pl.when((h >= 1) & (h < heads))
        def _():
            sibling_other_row(h)

    def event_2(h):
        done = h - 1

        @pl.when((h >= 1) & (h <= heads))
        def _():
            stage_a(done, yh).wait_recv()
            stage_c(done).wait_recv()
            total = acc_a[yh] + recv_a[done, yh].astype(F32) + recv_c[done].astype(F32)
            tot_b[...] = total
            send_b[done] = total.astype(BF16)
            for j in (0, 2, 1):
                stage_b(done, j).start()

        @pl.when(h == heads + 1)
        def _():
            cols = pl.ds(last * hd, hd)
            last_y().wait_recv()
            dk_ref[:, cols] = keep[last % 2, 0, yl] + recv_y[last, 0].astype(F32)
            for j in range(3):
                last_w(j).wait_recv()
            dv_ref[:, cols] = (
                tot_w[x] + recv_w[0].astype(F32) + recv_w[1].astype(F32) + recv_w[2].astype(F32)
            )

        @pl.when(h == 0)
        def _():
            forward_other_row(None)
            forward_other_row(0)
            masks(c, 1 - yh)

        @pl.when(h + 1 < heads)
        def _():
            forward_own_row(h + 1)

        @pl.when(h + 2 < heads)
        def _():
            send_own(h + 2)
            relay_across(h + 2)

    def event_3(h):
        done = h - 1

        odd = lax.rem(h + 1, 2)

        @pl.when(h == heads)
        def _():
            last_v().wait_recv()
            total = dv_acc[pl.ds(pl.multiple_of(yl * rows, rows), rows), :].reshape(4, 128, hd) + recv_v[...].astype(F32)
            tot_w[...] = total
            send_w[...] = total.astype(BF16)
            for j in (0, 2, 1):
                last_w(j).start()
            for j in range(3):
                last_x(j).wait_recv()
            for y in range(2):
                keep[odd, 0, y] = (
                    keep[odd, 0, y]
                    + recv_x[last, 0, 0, y].astype(F32)
                    + recv_x[last, 1, 0, y].astype(F32)
                    + recv_x[last, 2, 0, y].astype(F32)
                )
            send_y[last, 0] = keep[odd, 0, 1 - yl].astype(BF16)
            last_y().start()

        @pl.when((h >= 2) & (h <= heads))
        def _():
            cols = pl.ds(pl.multiple_of((h - 2) * hd, hd), hd)
            stage_y(h - 2).wait_recv()
            dk_ref[:, cols] = keep[lax.rem(h, 2), 0, yl] + recv_y[h - 2, 0].astype(F32)
            dv_ref[:, cols] = keep[lax.rem(h, 2), 1, yl] + recv_y[h - 2, 1].astype(F32)

        @pl.when(h == 0)
        def _():
            sibling_other_row(None)
            sibling_other_row(0)
            masks(1 - c, 1 - yh)

        @pl.when((h >= 1) & (h < heads))
        def _():
            exchange_rows(h)

        @pl.when((h >= 1) & (h + 1 < heads))
        def _():
            forward_other_row(h + 1)

    def compute(h, i):
        @pl.when((h == 0) & (i == 0))
        def _():
            for cp in kv_copies:
                cp.wait()

        @pl.when(i == 0)
        def _():
            kt[...] = k_all[h].T
            dk_acc[...] = jnp.zeros_like(dk_acc)
            dv_acc[...] = jnp.zeros_like(dv_acc)

        mine = jnp.where(h == 0, lax.rem(i, 2) == 0, i >= 2)
        own_row = jnp.where(h == 0, i < 2, (i == 0) | (i == 3))
        cc = jnp.where(mine, c, 1 - c)
        yy = jnp.where(own_row, yh, 1 - yh)
        at = pl.multiple_of((cc * 2 + yy) * rows, rows)
        q = qg[h, cc, yy, 0].reshape(rows, hd)
        g = qg[h, cc, yy, 1].reshape(rows, hd)
        norm = jnp.concatenate([nd[cc, yy, j, pl.ds(h, 1), :] for j in range(4)], axis=1) * LOG2E
        delta = jnp.concatenate([nd[cc, yy, j, pl.ds(heads + h, 1), :] for j in range(4)], axis=1)
        dqt = visit(scale, tile, q, g, norm, delta, k_all.at[h], v_all.at[h], kt[...], mask_ref, at,
                    dk_acc, dv_acc, sbuf)
        dq = dqt.T.reshape(4, 128, hd)

        @pl.when(mine)
        def _():
            acc_a[yy] = dq

        @pl.when(jnp.logical_not(mine))
        def _():
            send_a[h, yy] = dq.astype(BF16)
            stage_a(h, yy).start()

        @pl.when(i == 3)
        def _():
            for a, acc in enumerate((dk_acc, dv_acc)):
                send_x[h, a] = acc[...].reshape(2, 4, 128, hd).astype(BF16)
                for y in range(2):
                    keep[lax.rem(h, 2), a, y] = acc[pl.ds(pl.multiple_of((y * 4 + x) * 128, 128), 128), :]

    def step(n, carry):
        h = n // 4
        i = lax.rem(n, 4)
        for k, event in enumerate((event_0, event_1, event_2, event_3)):
            @pl.when(i == k)
            def _(event=event):
                event(h)

        @pl.when(h < heads)
        def _():
            compute(h, i)

        return carry

    lax.fori_loop(0, heads * 4 + 7, step, 0)

    def drain_reduce(h):
        for y in range(2):
            stage_a(h, y).wait_send()
        for j in range(3):
            stage_b(h, j).wait_send()
        stage_c(h).wait_send()

    def drain_gather(h, carry):
        for slot in range(15):
            gather(h, slot).wait_send()
        return carry

    def drain(h, carry):
        drain_reduce(h)
        for j in range(3):
            stage_x(h, j).wait_send()
        stage_y(h).wait_send()
        return carry

    for slot in range(15):
        gather(None, slot).wait_send()
        gather(0, slot).wait_send()
    lax.fori_loop(1, heads, drain_gather, 0)
    lax.fori_loop(0, last, drain, 0)
    drain_reduce(last)
    last_v().wait_send()
    last_y().wait_send()
    for j in range(3):
        last_x(j).wait_send()
        last_w(j).wait_send()


def finish(scale, dq_ref, dk_ref, dv_ref, q_out, k_out, v_out):
    q_out[...] = (dq_ref[...] * scale).astype(BF16)
    k_out[...] = (dk_ref[...] * scale).astype(BF16)
    v_out[...] = dv_ref[...].astype(BF16)


def shards(queries, out_grad, outputs, log_norms, src_keys, src_values, block_list, block_count, mask_bits):
    heads = log_norms.shape[0]
    local, features = queries.shape
    hd = features // heads
    n_src = src_keys.shape[0]
    tile = 256
    vmem = pl.BlockSpec(memory_space=pltpu.VMEM)
    anyspace = pl.BlockSpec(memory_space=pl.ANY)
    wide = jax.ShapeDtypeStruct((local, features), F32)
    narrow = jax.ShapeDtypeStruct((local, features), BF16)
    sums = pl.pallas_call(
        functools.partial(core, heads, tile),
        out_shape=(wide, wide, wide),
        in_specs=[pl.BlockSpec(memory_space=pltpu.SMEM), vmem] + [anyspace] * 7,
        out_specs=(vmem, vmem, vmem),
        scratch_shapes=[
            pltpu.VMEM(mask_bits.shape, jnp.int32),
            pltpu.VMEM((8, 128), jnp.int32),
            pltpu.SMEM((8, 128), jnp.int32),
            pltpu.VMEM((n_src, 16 * 128), F32),
            pltpu.VMEM((heads, 2, 2, 2, 4, 128, hd), BF16),
            pltpu.VMEM((heads, 128, hd), BF16),
            pltpu.VMEM((2, 2, 4, 2 * heads, 128), F32),
            pltpu.VMEM((heads, n_src, hd), BF16),
            pltpu.VMEM((heads, n_src, hd), BF16),
            pltpu.VMEM((hd, n_src), BF16),
            pltpu.VMEM((n_src, 512), BF16),
            pltpu.VMEM((n_src, hd), F32),
            pltpu.VMEM((n_src, hd), F32),
            pltpu.VMEM((heads, 2, 4, 128, hd), BF16),
            pltpu.VMEM((heads, 2, 4, 128, hd), BF16),
            pltpu.VMEM((2, 4, 128, hd), F32),
            pltpu.VMEM((heads, 4, 128, hd), BF16),
            pltpu.VMEM((heads, 4, 128, hd), BF16),
            pltpu.VMEM((4, 128, hd), F32),
            pltpu.VMEM((heads, 4, 128, hd), BF16),
            pltpu.VMEM((heads, 3, 128, hd), BF16),
            pltpu.VMEM((heads, 2, 2, 4, 128, hd), BF16),
            pltpu.VMEM((heads, 3, 2, 2, 128, hd), BF16),
            pltpu.VMEM((2, 2, 2, 128, hd), F32),
            pltpu.VMEM((heads, 2, 128, hd), BF16),
            pltpu.VMEM((heads, 2, 128, hd), BF16),
            pltpu.VMEM((4, 128, hd), BF16),
            pltpu.VMEM((4, 128, hd), F32),
            pltpu.VMEM((4, 128, hd), BF16),
            pltpu.VMEM((3, 128, hd), BF16),
            pltpu.SemaphoreType.DMA((heads, 5)),
            pltpu.SemaphoreType.DMA((3,)),
            pltpu.SemaphoreType.DMA((heads, 17)),
            pltpu.SemaphoreType.DMA((heads, 17)),
            pltpu.SemaphoreType.DMA((15,)),
            pltpu.SemaphoreType.DMA((15,)),
            pltpu.SemaphoreType.DMA((heads, 14)),
            pltpu.SemaphoreType.DMA((heads, 14)),
        ],
        compiler_params=pltpu.CompilerParams(
            vmem_limit_bytes=67043328, collective_id=0, has_side_effects=True
        ),
        name="attention",
    )(block_count, block_list, mask_bits, queries, out_grad, outputs, log_norms, src_keys, src_values)
    return pl.pallas_call(
        functools.partial(finish, hd ** -0.5),
        out_shape=(narrow, narrow, narrow),
        in_specs=[vmem] * 3,
        out_specs=(vmem, vmem, vmem),
        name="finish",
    )(*sums)


def solution(mesh):
    rows = P(("src", "rep"), None)
    placed = (
        rows,
        rows,
        rows,
        P(None, ("src", "rep")),
        P("src", None),
        P("src", None),
        P("src", "rep", None, None),
        P("src", "rep"),
        P("src", "rep", None, None, None),
    )
    return jax.shard_map(shards, mesh=mesh, in_specs=placed, out_specs=(rows, rows, rows), check_vma=False)
```

```python
import functools
import math

import jax
import jax.numpy as jnp
from jax import lax
from jax.experimental import pallas as pl
from jax.experimental.pallas import tpu as pltpu
from jax.sharding import PartitionSpec as P

F32 = jnp.float32
BF16 = jnp.bfloat16
LOG2E = math.log2(math.e)
MESH = pl.DeviceIdType.MESH


def nt_dot(a, b):
    return lax.dot_general(a, b, (((1,), (1,)), ((), ())), preferred_element_type=F32)


def nn_dot(a, b):
    return lax.dot_general(a, b, (((1,), (0,)), ((), ())), preferred_element_type=F32)


def tn_dot(a, b):
    return lax.dot_general(a, b, (((0,), (0,)), ((), ())), preferred_element_type=F32)


def build_masks(u, dest, src_blocks, table, words_ref, mask_ref):
    row = lax.broadcasted_iota(jnp.int32, (16, 128), 0)
    lane = lax.broadcasted_iota(jnp.int32, (16, 128), 1)
    half = jnp.where(lax.rem(lane, 16) >= 8, 8, 0)
    spread = jnp.where(row == lane // 16 + half, 1.0, 0.0).astype(BF16)
    bit = jnp.left_shift(1, lax.rem(lax.broadcasted_iota(jnp.int32, (1, 128), 1), 8))
    words = jnp.concatenate(
        [
            words_ref[0, 0, jnp.clip(table[0, dest * src_blocks + j], 0, words_ref.shape[2] - 1)] * table[1, dest * src_blocks + j]
            for j in range(src_blocks)
        ],
        axis=1,
    )
    halves = jnp.concatenate(
        [jnp.bitwise_and(words, 255), jnp.bitwise_and(jnp.right_shift(words, 8), 255)], axis=0
    )
    wide = tn_dot(halves.astype(F32).astype(BF16), spread).astype(jnp.int32)
    picked = jnp.where(jnp.bitwise_and(wide, bit) != 0, 1.0, 0.0)
    mask_ref[:, pl.ds(pl.multiple_of(u * 128, 128), 128)] = picked


def visit(scale, tile, q, g, norm, delta, k_ref, v_ref, kt, mask_ref, at, dk_ref, dv_ref, sbuf):
    n_src = k_ref.shape[0]
    rows = q.shape[0]
    for c in range(n_src // tile):
        cs = pl.ds(c * tile, tile)
        s = nt_dot(k_ref[cs, :], q)
        e = jnp.exp2(s * (scale * LOG2E) - norm)
        p = e * mask_ref[cs, pl.ds(at, rows)]
        d = nt_dot(v_ref[cs, :], g)
        ds = p * (d - delta)
        p_low = p.astype(BF16)
        s_low = ds.astype(BF16)
        sbuf[cs, :] = s_low
        dv_ref[cs, :] += nn_dot(p_low, g)
        dk_ref[cs, :] += nn_dot(s_low, q)
    return nn_dot(kt, sbuf[...])


def pair_slots(list_ref, count, src_blocks, n_pairs):
    capacity = list_ref.shape[3]
    code = list_ref[0, 0, 0:1, :] * src_blocks + list_ref[0, 0, 1:2, :]
    order = lax.broadcasted_iota(jnp.int32, (n_pairs, capacity), 1)
    pair = lax.broadcasted_iota(jnp.int32, (n_pairs, capacity), 0)
    hit = (code == pair) & (order < count)
    slot = jnp.sum(jnp.where(hit, order, 0), axis=1, keepdims=True)
    live = jnp.sum(jnp.where(hit, 1, 0), axis=1, keepdims=True)
    column = lax.broadcasted_iota(jnp.int32, (n_pairs, 128), 1)
    both = jnp.where(column == 0, slot, jnp.where(column == 1, live, 0))
    return both.T[0:8]


def core(heads, tile, count_ref, list_ref, words_hbm, q_hbm, g_hbm, o_hbm, norm_hbm, k_hbm, v_hbm,
         out_ref,
         words, slots, table, mask_ref, qg, o_all, nd, k_all, v_all, kt, sbuf, dk_acc, dv_acc,
         send_a, recv_a, acc_a, send_c, recv_c, tot_b, send_b, recv_b,
         send_x, recv_x, keep, send_y, recv_y, recv_v, tot_w, send_w, recv_w,
         local_sem, extra_sem, ag_send, ag_recv, nd_send, nd_recv, rs_send, rs_recv):
    dq_ref, dk_ref, dv_ref = out_ref.at[0], out_ref.at[1], out_ref.at[2]
    hd = kt.shape[0]
    n_src = kt.shape[1]
    src_blocks = n_src // 128
    rows = 4 * 128
    scale = hd ** -0.5
    src, rep = lax.axis_index("src"), lax.axis_index("rep")
    yh, z, c = src // 8, lax.rem(src, 8) // 2, lax.rem(src, 2)
    yl, x = rep // 4, lax.rem(rep, 4)

    def at_src(yy, zz, cc):
        return {"src": yy * 8 + zz * 2 + cc, "rep": rep}

    def at_rep(yy, xx):
        return {"src": src, "rep": yy * 4 + xx}

    sibling = at_src(yh, z, 1 - c)
    across = at_src(1 - yh, z, c)
    zs = [lax.rem(z + d, 4) for d in (1, 2, 3)]
    xs = [lax.rem(x + d, 4) for d in (1, 2, 3)]
    around = [at_src(yh, zz, c) for zz in zs]
    beside = [at_rep(yl, xx) for xx in xs]
    over = at_rep(1 - yl, x)

    barrier = pltpu.get_barrier_semaphore()
    for peer in [sibling, across, over] + around + beside:
        pl.semaphore_signal(barrier, inc=1, device_id=peer, device_id_type=MESH)

    mine_copies, kv_copies = [], []
    for h in range(heads):
        cols = pl.ds(h * hd, hd)
        for i, (a, b) in enumerate((
            (q_hbm, qg.at[h, c, yh, 0, z]), (g_hbm, qg.at[h, c, yh, 1, z]), (o_hbm, o_all.at[h]),
            (k_hbm, k_all.at[h]), (v_hbm, v_all.at[h]),
        )):
            cp = pltpu.make_async_copy(a.at[:, cols], b, local_sem.at[h, i])
            if i < 3:
                cp.start()
                mine_copies.append(cp)
            else:
                kv_copies.append(cp)
    norm_copy = pltpu.make_async_copy(norm_hbm, nd.at[c, yh, z, pl.ds(0, heads)], extra_sem.at[0])
    norm_copy.start()
    words_copy = pltpu.make_async_copy(words_hbm, words, extra_sem.at[1])
    words_copy.start()
    for cp in kv_copies:
        cp.start()

    slots[...] = pair_slots(list_ref, count_ref[0, 0], src_blocks, 128)
    table_copy = pltpu.make_async_copy(slots, table, extra_sem.at[2])
    table_copy.start()

    def remote(a, b, s, r, peer):
        return pltpu.make_async_remote_copy(
            src_ref=a, dst_ref=b, send_sem=s, recv_sem=r, device_id=peer, device_id_type=MESH
        )

    def gather_copy(h, cc, yy, zz, slot, peer):
        if h is None:
            ref = nd.at[cc, yy, zz]
            return remote(ref, ref, nd_send.at[slot], nd_recv.at[slot], peer)
        ref = qg.at[h, cc, yy, :, zz]
        return remote(ref, ref, ag_send.at[h, slot], ag_recv.at[h, slot], peer)

    def gather(h, slot):
        if slot == 0:
            yy, zz, peer = yh, z, across
        elif slot < 4:
            yy, zz, peer = yh, z, around[slot - 1]
        elif slot < 7:
            yy, zz, peer = 1 - yh, z, around[slot - 4]
        elif slot == 7:
            yy, zz, peer = yh, z, sibling
        elif slot == 8:
            yy, zz, peer = 1 - yh, z, sibling
        elif slot < 12:
            yy, zz, peer = yh, zs[slot - 9], sibling
        else:
            yy, zz, peer = 1 - yh, zs[slot - 12], sibling
        return gather_copy(h, c, yy, zz, slot, peer)

    def arrived(h, slot):
        if slot == 0:
            cc, yy, zz = c, 1 - yh, z
        elif slot < 4:
            cc, yy, zz = c, yh, zs[3 - slot]
        elif slot < 7:
            cc, yy, zz = c, 1 - yh, zs[6 - slot]
        elif slot == 7:
            cc, yy, zz = 1 - c, yh, z
        elif slot == 8:
            cc, yy, zz = 1 - c, 1 - yh, z
        elif slot < 12:
            cc, yy, zz = 1 - c, yh, zs[slot - 9]
        else:
            cc, yy, zz = 1 - c, 1 - yh, zs[slot - 12]
        gather_copy(h, cc, yy, zz, slot, sibling).wait_recv()

    def send_own(h):
        for slot in (1, 3, 2, 7):
            gather(h, slot).start()

    def relay_across(h):
        arrived(h, 0)
        for slot in (4, 6, 5, 8):
            gather(h, slot).start()

    def forward_own_row(h):
        for d in (1, 3, 2):
            arrived(h, d)
            gather(h, 12 - d).start()

    def forward_other_row(h):
        for d in (1, 3, 2):
            arrived(h, 3 + d)
            gather(h, 15 - d).start()

    def half(h, yy, zz, part, slot, peer):
        ref = qg.at[h, c, yy, part, zz]
        return remote(ref, ref, ag_send.at[h, slot], ag_recv.at[h, slot], peer)

    def ring_own(h):
        for slot in (1, 3, 7):
            gather(h, slot).start()

    def ring_across(h):
        arrived(h, 0)
        for slot in (4, 6, 8):
            gather(h, slot).start()

    def ring_halves(h):
        return [
            (1, 11, half(h, yh, zs[2], 0, 2, around[0])),
            (3, 9, half(h, yh, zs[0], 1, 15, around[2])),
            (4, 14, half(h, 1 - yh, zs[2], 0, 5, around[0])),
            (6, 12, half(h, 1 - yh, zs[0], 1, 16, around[2])),
        ]

    def ring_forward(h):
        for slot, core_slot, onward in ring_halves(h):
            arrived(h, slot)
            onward.start()
            gather(h, core_slot).start()

    def ring_finish(h):
        for yy, slots_, core_slot in ((yh, (2, 15), 10), (1 - yh, (5, 16), 13)):
            for part in range(2):
                half(h, yy, zs[1], part, slots_[part], sibling).wait_recv()
            gather(h, core_slot).start()

    def sibling_own_row(h):
        for slot in (7, 9, 10, 11):
            arrived(h, slot)

    def sibling_other_row(h):
        for slot in (8, 12, 13, 14):
            arrived(h, slot)

    def stage_a(h, y):
        return remote(send_a.at[h, y], recv_a.at[h, y], rs_send.at[h, y], rs_recv.at[h, y], sibling)

    def stage_c(h):
        return remote(send_c.at[h], recv_c.at[h], rs_send.at[h, 2], rs_recv.at[h, 2], across)

    def stage_b(h, j):
        return remote(send_b.at[h, zs[j]], recv_b.at[h, j], rs_send.at[h, 3 + j], rs_recv.at[h, 3 + j], around[j])

    def stage_x(h, j):
        return remote(send_x.at[h, :, :, xs[j]], recv_x.at[h, j], rs_send.at[h, 6 + j], rs_recv.at[h, 6 + j], beside[j])

    def stage_y(h):
        return remote(send_y.at[h], recv_y.at[h], rs_send.at[h, 9], rs_recv.at[h, 9], over)

    last = heads - 1

    def last_x(j):
        return remote(send_x.at[last, 0, :, xs[j]], recv_x.at[last, j, 0], rs_send.at[last, 6 + j],
                      rs_recv.at[last, 6 + j], beside[j])

    def last_y():
        return remote(send_y.at[last, 0], recv_y.at[last, 0], rs_send.at[last, 9], rs_recv.at[last, 9], over)

    def last_v():
        return remote(send_x.at[last, 1, 1 - yl], recv_v, rs_send.at[last, 10], rs_recv.at[last, 10], over)

    def last_w(j):
        return remote(send_w.at[xs[j]], recv_w.at[j], rs_send.at[last, 11 + j], rs_recv.at[last, 11 + j], beside[j])

    def masks(cc, yy):
        for zz in range(4):
            build_masks((cc * 2 + yy) * 4 + zz, yy * 8 + zz * 2 + cc, src_blocks, table, words, mask_ref)

    for cp in mine_copies[:2]:
        cp.wait()
    pl.semaphore_wait(barrier, 9)
    send_own(0)
    gather(0, 0).start()
    norm_copy.wait()
    for cp in mine_copies[2:]:
        cp.wait()
    for h in range(heads):
        product = qg[h, c, yh, 1, z].astype(F32) * o_all[h].astype(F32)
        nd[c, yh, z, heads + h : heads + h + 1, :] = jnp.sum(product.T, axis=0, keepdims=True)
    send_own(None)
    gather(None, 0).start()
    for h in range(1, heads):
        gather(h, 0).start()
    words_copy.wait()
    table_copy.wait()
    masks(c, yh)
    relay_across(0)
    relay_across(None)
    masks(1 - c, yh)
    masks(c, 1 - yh)
    masks(1 - c, 1 - yh)
    forward_own_row(0)
    forward_own_row(None)

    def exchange_rows(h):
        stage_a(h, 1 - yh).wait_recv()
        send_c[h] = (acc_a[1 - yh] + recv_a[h, 1 - yh].astype(F32)).astype(BF16)
        stage_c(h).start()

    def event_0(h):
        done = h - 1

        @pl.when((h >= 1) & (h < heads))
        def _():
            for j in (0, 2, 1):
                stage_x(done, j).start()

        @pl.when(h == heads)
        def _():
            last_v().start()
            for j in (0, 2, 1):
                last_x(j).start()

        @pl.when(h == 1)
        def _():
            exchange_rows(0)

        @pl.when(h == 0)
        def _():
            send_own(1)
            relay_across(1)

        @pl.when(h == 1)
        def _():
            forward_other_row(1)

        @pl.when((h >= 1) & (h < heads))
        def _():
            sibling_own_row(h)

        @pl.when((h >= 2) & (h <= heads))
        def _():
            for j in range(3):
                stage_x(h - 2, j).wait_recv()
            for a in range(2):
                for y in range(2):
                    keep[lax.rem(h, 2), a, y] = (
                        keep[lax.rem(h, 2), a, y]
                        + recv_x[h - 2, 0, a, y].astype(F32)
                        + recv_x[h - 2, 1, a, y].astype(F32)
                        + recv_x[h - 2, 2, a, y].astype(F32)
                    )
                send_y[h - 2, a] = keep[lax.rem(h, 2), a, 1 - yl].astype(BF16)
            stage_y(h - 2).start()

    def event_1(h):
        @pl.when(h >= 2)
        def _():
            cols = pl.ds(pl.multiple_of((h - 2) * hd, hd), hd)
            for j in range(3):
                stage_b((h - 2), j).wait_recv()
            total = (
                tot_b[z]
                + recv_b[(h - 2), 0].astype(F32)
                + recv_b[(h - 2), 1].astype(F32)
                + recv_b[(h - 2), 2].astype(F32)
            )
            dq_ref[:, cols] = (total * scale).T.astype(BF16)

        @pl.when(h == 0)
        def _():
            sibling_own_row(None)
            sibling_own_row(0)

        @pl.when((h >= 1) & (h < heads))
        def _():
            sibling_other_row(h)

    def event_2(h):
        done = h - 1

        @pl.when((h >= 1) & (h <= heads))
        def _():
            stage_a(done, yh).wait_recv()
            stage_c(done).wait_recv()
            total = acc_a[yh] + recv_a[done, yh].astype(F32) + recv_c[done].astype(F32)
            tot_b[...] = total
            send_b[done] = total.astype(BF16)
            for j in (0, 2, 1):
                stage_b(done, j).start()

        @pl.when(h == heads + 1)
        def _():
            cols = pl.ds(last * hd, hd)
            last_y().wait_recv()
            dk_ref[:, cols] = ((keep[last % 2, 0, yl] + recv_y[last, 0].astype(F32)) * scale).astype(BF16)
            for j in range(3):
                last_w(j).wait_recv()
            dv_ref[:, cols] = (
                tot_w[x] + recv_w[0].astype(F32) + recv_w[1].astype(F32) + recv_w[2].astype(F32)
            ).astype(BF16)

        @pl.when(h == 0)
        def _():
            forward_other_row(None)
            forward_other_row(0)

        @pl.when(h + 1 < heads)
        def _():
            forward_own_row(h + 1)

        @pl.when(h + 2 < heads)
        def _():
            send_own(h + 2)
            relay_across(h + 2)

    def event_3(h):
        done = h - 1

        odd = lax.rem(h + 1, 2)

        @pl.when(h == heads)
        def _():
            last_v().wait_recv()
            total = dv_acc[pl.ds(pl.multiple_of(yl * rows, rows), rows), :].reshape(4, 128, hd) + recv_v[...].astype(F32)
            tot_w[...] = total
            send_w[...] = total.astype(BF16)
            for j in (0, 2, 1):
                last_w(j).start()
            for j in range(3):
                last_x(j).wait_recv()
            for y in range(2):
                keep[odd, 0, y] = (
                    keep[odd, 0, y]
                    + recv_x[last, 0, 0, y].astype(F32)
                    + recv_x[last, 1, 0, y].astype(F32)
                    + recv_x[last, 2, 0, y].astype(F32)
                )
            send_y[last, 0] = keep[odd, 0, 1 - yl].astype(BF16)
            last_y().start()

        @pl.when((h >= 2) & (h <= heads))
        def _():
            cols = pl.ds(pl.multiple_of((h - 2) * hd, hd), hd)
            stage_y(h - 2).wait_recv()
            dk_ref[:, cols] = ((keep[lax.rem(h, 2), 0, yl] + recv_y[h - 2, 0].astype(F32)) * scale).astype(BF16)
            dv_ref[:, cols] = (keep[lax.rem(h, 2), 1, yl] + recv_y[h - 2, 1].astype(F32)).astype(BF16)

        @pl.when(h == 0)
        def _():
            sibling_other_row(None)
            sibling_other_row(0)

        @pl.when((h >= 1) & (h < heads))
        def _():
            exchange_rows(h)

        @pl.when((h >= 1) & (h + 1 < heads))
        def _():
            forward_other_row(h + 1)

    def compute(h, i):
        @pl.when((h == 0) & (i == 0))
        def _():
            for cp in kv_copies:
                cp.wait()

        @pl.when(i == 0)
        def _():
            kt[...] = k_all[h].T
            dk_acc[...] = jnp.zeros_like(dk_acc)
            dv_acc[...] = jnp.zeros_like(dv_acc)

        mine = jnp.where(h == 0, lax.rem(i, 2) == 0, i >= 2)
        own_row = jnp.where(h == 0, i < 2, (i == 0) | (i == 3))
        cc = jnp.where(mine, c, 1 - c)
        yy = jnp.where(own_row, yh, 1 - yh)
        at = pl.multiple_of((cc * 2 + yy) * rows, rows)
        q = qg[h, cc, yy, 0].reshape(rows, hd)
        g = qg[h, cc, yy, 1].reshape(rows, hd)
        norm = jnp.concatenate([nd[cc, yy, j, pl.ds(h, 1), :] for j in range(4)], axis=1) * LOG2E
        delta = jnp.concatenate([nd[cc, yy, j, pl.ds(heads + h, 1), :] for j in range(4)], axis=1)
        dqt = visit(scale, tile, q, g, norm, delta, k_all.at[h], v_all.at[h], kt[...], mask_ref, at,
                    dk_acc, dv_acc, sbuf)

        @pl.when(mine)
        def _():
            for j in range(4):
                acc_a[yy, j] = dqt[:, j * 128 : (j + 1) * 128]

        @pl.when(jnp.logical_not(mine))
        def _():
            for j in range(4):
                send_a[h, yy, j] = dqt[:, j * 128 : (j + 1) * 128].astype(BF16)
            stage_a(h, yy).start()

        @pl.when(i == 3)
        def _():
            for a, acc in enumerate((dk_acc, dv_acc)):
                send_x[h, a] = acc[...].reshape(2, 4, 128, hd).astype(BF16)
                for y in range(2):
                    keep[lax.rem(h, 2), a, y] = acc[pl.ds(pl.multiple_of((y * 4 + x) * 128, 128), 128), :]

    def step(n, carry):
        h = n // 4
        i = lax.rem(n, 4)
        for k, event in enumerate((event_0, event_1, event_2, event_3)):
            @pl.when(i == k)
            def _(event=event):
                event(h)

        @pl.when(h < heads)
        def _():
            compute(h, i)

        return carry

    lax.fori_loop(0, heads * 4 + 7, step, 0)

    def drain_reduce(h):
        for y in range(2):
            stage_a(h, y).wait_send()
        for j in range(3):
            stage_b(h, j).wait_send()
        stage_c(h).wait_send()

    def drain_gather(h, carry):
        for slot in range(15):
            gather(h, slot).wait_send()
        return carry

    def drain(h, carry):
        drain_reduce(h)
        for j in range(3):
            stage_x(h, j).wait_send()
        stage_y(h).wait_send()
        return carry

    for slot in range(15):
        gather(None, slot).wait_send()
        gather(0, slot).wait_send()
    lax.fori_loop(1, heads, drain_gather, 0)
    lax.fori_loop(0, last, drain, 0)
    drain_reduce(last)
    last_v().wait_send()
    last_y().wait_send()
    for j in range(3):
        last_x(j).wait_send()
        last_w(j).wait_send()


def finish(sums_ref, q_out, k_out, v_out):
    for i, out in enumerate((q_out, k_out, v_out)):
        out[...] = sums_ref[i]


def shards(queries, out_grad, outputs, log_norms, src_keys, src_values, block_list, block_count, mask_bits):
    heads = log_norms.shape[0]
    local, features = queries.shape
    hd = features // heads
    n_src = src_keys.shape[0]
    tile = 256
    vmem = pl.BlockSpec(memory_space=pltpu.VMEM)
    anyspace = pl.BlockSpec(memory_space=pl.ANY)
    narrow = jax.ShapeDtypeStruct((local, features), BF16)
    sums = pl.pallas_call(
        functools.partial(core, heads, tile),
        out_shape=jax.ShapeDtypeStruct((3, local, features), BF16),
        in_specs=[pl.BlockSpec(memory_space=pltpu.SMEM), vmem] + [anyspace] * 7,
        out_specs=vmem,
        scratch_shapes=[
            pltpu.VMEM(mask_bits.shape, jnp.int32),
            pltpu.VMEM((8, 128), jnp.int32),
            pltpu.SMEM((8, 128), jnp.int32),
            pltpu.VMEM((n_src, 16 * 128), F32),
            pltpu.VMEM((heads, 2, 2, 2, 4, 128, hd), BF16),
            pltpu.VMEM((heads, 128, hd), BF16),
            pltpu.VMEM((2, 2, 4, 2 * heads, 128), F32),
            pltpu.VMEM((heads, n_src, hd), BF16),
            pltpu.VMEM((heads, n_src, hd), BF16),
            pltpu.VMEM((hd, n_src), BF16),
            pltpu.VMEM((n_src, 512), BF16),
            pltpu.VMEM((n_src, hd), F32),
            pltpu.VMEM((n_src, hd), F32),
            pltpu.VMEM((heads, 2, 4, hd, 128), BF16),
            pltpu.VMEM((heads, 2, 4, hd, 128), BF16),
            pltpu.VMEM((2, 4, hd, 128), F32),
            pltpu.VMEM((heads, 4, hd, 128), BF16),
            pltpu.VMEM((heads, 4, hd, 128), BF16),
            pltpu.VMEM((4, hd, 128), F32),
            pltpu.VMEM((heads, 4, hd, 128), BF16),
            pltpu.VMEM((heads, 3, hd, 128), BF16),
            pltpu.VMEM((heads, 2, 2, 4, 128, hd), BF16),
            pltpu.VMEM((heads, 3, 2, 2, 128, hd), BF16),
            pltpu.VMEM((2, 2, 2, 128, hd), F32),
            pltpu.VMEM((heads, 2, 128, hd), BF16),
            pltpu.VMEM((heads, 2, 128, hd), BF16),
            pltpu.VMEM((4, 128, hd), BF16),
            pltpu.VMEM((4, 128, hd), F32),
            pltpu.VMEM((4, 128, hd), BF16),
            pltpu.VMEM((3, 128, hd), BF16),
            pltpu.SemaphoreType.DMA((heads, 5)),
            pltpu.SemaphoreType.DMA((3,)),
            pltpu.SemaphoreType.DMA((heads, 17)),
            pltpu.SemaphoreType.DMA((heads, 17)),
            pltpu.SemaphoreType.DMA((15,)),
            pltpu.SemaphoreType.DMA((15,)),
            pltpu.SemaphoreType.DMA((heads, 14)),
            pltpu.SemaphoreType.DMA((heads, 14)),
        ],
        compiler_params=pltpu.CompilerParams(
            vmem_limit_bytes=67043328, collective_id=0, has_side_effects=True
        ),
        name="attention",
    )(block_count, block_list, mask_bits, queries, out_grad, outputs, log_norms, src_keys, src_values)
    return pl.pallas_call(
        finish,
        out_shape=(narrow, narrow, narrow),
        in_specs=[vmem],
        out_specs=(vmem, vmem, vmem),
        name="finish",
    )(sums)


def solution(mesh):
    rows = P(("src", "rep"), None)
    placed = (
        rows,
        rows,
        rows,
        P(None, ("src", "rep")),
        P("src", None),
        P("src", None),
        P("src", "rep", None, None),
        P("src", "rep"),
        P("src", "rep", None, None, None),
    )
    return jax.shard_map(shards, mesh=mesh, in_specs=placed, out_specs=(rows, rows, rows), check_vma=False)
```

```python
import functools
import math

import jax
import jax.numpy as jnp
from jax import lax
from jax.experimental import pallas as pl
from jax.experimental.pallas import tpu as pltpu
from jax.sharding import PartitionSpec as P

F32 = jnp.float32
BF16 = jnp.bfloat16
LOG2E = math.log2(math.e)
MESH = pl.DeviceIdType.MESH


def nt_dot(a, b):
    return lax.dot_general(a, b, (((1,), (1,)), ((), ())), preferred_element_type=F32)


def nn_dot(a, b):
    return lax.dot_general(a, b, (((1,), (0,)), ((), ())), preferred_element_type=F32)


def tn_dot(a, b):
    return lax.dot_general(a, b, (((0,), (0,)), ((), ())), preferred_element_type=F32)


def build_masks(u, dest, src_blocks, table, words_ref, mask_ref):
    row = lax.broadcasted_iota(jnp.int32, (16, 128), 0)
    lane = lax.broadcasted_iota(jnp.int32, (16, 128), 1)
    half = jnp.where(lax.rem(lane, 16) >= 8, 8, 0)
    spread = jnp.where(row == lane // 16 + half, 1.0, 0.0).astype(BF16)
    bit = jnp.left_shift(1, lax.rem(lax.broadcasted_iota(jnp.int32, (1, 128), 1), 8))
    words = jnp.concatenate(
        [
            words_ref[0, 0, jnp.clip(table[0, dest * src_blocks + j], 0, words_ref.shape[2] - 1)] * table[1, dest * src_blocks + j]
            for j in range(src_blocks)
        ],
        axis=1,
    )
    halves = jnp.concatenate(
        [jnp.bitwise_and(words, 255), jnp.bitwise_and(jnp.right_shift(words, 8), 255)], axis=0
    )
    wide = tn_dot(halves.astype(F32).astype(BF16), spread).astype(jnp.int32)
    picked = jnp.where(jnp.bitwise_and(wide, bit) != 0, 0.0, -1e30)
    mask_ref[:, pl.ds(pl.multiple_of(u * 128, 128), 128)] = picked


def visit(scale, tile, q, g, norm, delta, k_ref, v_ref, kt, mask_ref, at, dk_ref, dv_ref, sbuf):
    n_src = k_ref.shape[0]
    rows = q.shape[0]
    for c in range(n_src // tile):
        cs = pl.ds(c * tile, tile)
        s = nt_dot(k_ref[cs, :], q)
        p = jnp.exp2((s * (scale * LOG2E) - norm) + mask_ref[cs, pl.ds(at, rows)])
        d = nt_dot(v_ref[cs, :], g)
        ds = p * (d - delta)
        p_low = p.astype(BF16)
        s_low = ds.astype(BF16)
        sbuf[cs, :] = s_low
        dv_ref[cs, :] += nn_dot(p_low, g)
        dk_ref[cs, :] += nn_dot(s_low, q)
    return nn_dot(kt, sbuf[...])


def pair_slots(list_ref, count, src_blocks, n_pairs):
    capacity = list_ref.shape[3]
    code = list_ref[0, 0, 0:1, :] * src_blocks + list_ref[0, 0, 1:2, :]
    order = lax.broadcasted_iota(jnp.int32, (n_pairs, capacity), 1)
    pair = lax.broadcasted_iota(jnp.int32, (n_pairs, capacity), 0)
    hit = (code == pair) & (order < count)
    slot = jnp.sum(jnp.where(hit, order, 0), axis=1, keepdims=True)
    live = jnp.sum(jnp.where(hit, 1, 0), axis=1, keepdims=True)
    column = lax.broadcasted_iota(jnp.int32, (n_pairs, 128), 1)
    both = jnp.where(column == 0, slot, jnp.where(column == 1, live, 0))
    return both.T[0:8]


def core(heads, tile, count_ref, list_ref, words_hbm, q_hbm, g_hbm, o_hbm, norm_hbm, k_hbm, v_hbm,
         out_ref,
         words, slots, table, mask_ref, qg, o_all, nd, k_all, v_all, kt, sbuf, dk_acc, dv_acc,
         send_a, recv_a, acc_a, send_c, recv_c, tot_b, send_b, recv_b,
         send_x, recv_x, keep, send_y, recv_y, recv_v, tot_w, send_w, recv_w,
         local_sem, extra_sem, ag_send, ag_recv, nd_send, nd_recv, rs_send, rs_recv):
    dq_ref, dk_ref, dv_ref = out_ref.at[0], out_ref.at[1], out_ref.at[2]
    hd = kt.shape[0]
    n_src = kt.shape[1]
    src_blocks = n_src // 128
    rows = 4 * 128
    scale = hd ** -0.5
    src, rep = lax.axis_index("src"), lax.axis_index("rep")
    yh, z, c = src // 8, lax.rem(src, 8) // 2, lax.rem(src, 2)
    yl, x = rep // 4, lax.rem(rep, 4)

    def at_src(yy, zz, cc):
        return {"src": yy * 8 + zz * 2 + cc, "rep": rep}

    def at_rep(yy, xx):
        return {"src": src, "rep": yy * 4 + xx}

    sibling = at_src(yh, z, 1 - c)
    across = at_src(1 - yh, z, c)
    zs = [lax.rem(z + d, 4) for d in (1, 2, 3)]
    xs = [lax.rem(x + d, 4) for d in (1, 2, 3)]
    around = [at_src(yh, zz, c) for zz in zs]
    beside = [at_rep(yl, xx) for xx in xs]
    over = at_rep(1 - yl, x)

    barrier = pltpu.get_barrier_semaphore()
    for peer in [sibling, across, over] + around + beside:
        pl.semaphore_signal(barrier, inc=1, device_id=peer, device_id_type=MESH)

    mine_copies, kv_copies = [], []
    for h in range(heads):
        cols = pl.ds(h * hd, hd)
        for i, (a, b) in enumerate((
            (q_hbm, qg.at[h, c, yh, 0, z]), (g_hbm, qg.at[h, c, yh, 1, z]), (o_hbm, o_all.at[h]),
            (k_hbm, k_all.at[h]), (v_hbm, v_all.at[h]),
        )):
            cp = pltpu.make_async_copy(a.at[:, cols], b, local_sem.at[h, i])
            if i < 3:
                cp.start()
                mine_copies.append(cp)
            else:
                kv_copies.append(cp)
    norm_copy = pltpu.make_async_copy(norm_hbm, nd.at[c, yh, z, pl.ds(0, heads)], extra_sem.at[0])
    norm_copy.start()
    words_copy = pltpu.make_async_copy(words_hbm, words, extra_sem.at[1])
    words_copy.start()
    for cp in kv_copies:
        cp.start()

    slots[...] = pair_slots(list_ref, count_ref[0, 0], src_blocks, 128)
    table_copy = pltpu.make_async_copy(slots, table, extra_sem.at[2])
    table_copy.start()

    def remote(a, b, s, r, peer):
        return pltpu.make_async_remote_copy(
            src_ref=a, dst_ref=b, send_sem=s, recv_sem=r, device_id=peer, device_id_type=MESH
        )

    def gather_copy(h, cc, yy, zz, slot, peer):
        if h is None:
            ref = nd.at[cc, yy, zz]
            return remote(ref, ref, nd_send.at[slot], nd_recv.at[slot], peer)
        ref = qg.at[h, cc, yy, :, zz]
        return remote(ref, ref, ag_send.at[h, slot], ag_recv.at[h, slot], peer)

    def gather(h, slot):
        if slot == 0:
            yy, zz, peer = yh, z, across
        elif slot < 4:
            yy, zz, peer = yh, z, around[slot - 1]
        elif slot < 7:
            yy, zz, peer = 1 - yh, z, around[slot - 4]
        elif slot == 7:
            yy, zz, peer = yh, z, sibling
        elif slot == 8:
            yy, zz, peer = 1 - yh, z, sibling
        elif slot < 12:
            yy, zz, peer = yh, zs[slot - 9], sibling
        else:
            yy, zz, peer = 1 - yh, zs[slot - 12], sibling
        return gather_copy(h, c, yy, zz, slot, peer)

    def arrived(h, slot):
        if slot == 0:
            cc, yy, zz = c, 1 - yh, z
        elif slot < 4:
            cc, yy, zz = c, yh, zs[3 - slot]
        elif slot < 7:
            cc, yy, zz = c, 1 - yh, zs[6 - slot]
        elif slot == 7:
            cc, yy, zz = 1 - c, yh, z
        elif slot == 8:
            cc, yy, zz = 1 - c, 1 - yh, z
        elif slot < 12:
            cc, yy, zz = 1 - c, yh, zs[slot - 9]
        else:
            cc, yy, zz = 1 - c, 1 - yh, zs[slot - 12]
        gather_copy(h, cc, yy, zz, slot, sibling).wait_recv()

    def send_own(h):
        for slot in (1, 3, 2, 7):
            gather(h, slot).start()

    def relay_across(h):
        arrived(h, 0)
        for slot in (4, 6, 5, 8):
            gather(h, slot).start()

    def forward_own_row(h):
        for d in (1, 3, 2):
            arrived(h, d)
            gather(h, 12 - d).start()

    def forward_other_row(h):
        for d in (1, 3, 2):
            arrived(h, 3 + d)
            gather(h, 15 - d).start()

    def half(h, yy, zz, part, slot, peer):
        ref = qg.at[h, c, yy, part, zz]
        return remote(ref, ref, ag_send.at[h, slot], ag_recv.at[h, slot], peer)

    def ring_own(h):
        for slot in (1, 3, 7):
            gather(h, slot).start()

    def ring_across(h):
        arrived(h, 0)
        for slot in (4, 6, 8):
            gather(h, slot).start()

    def ring_halves(h):
        return [
            (1, 11, half(h, yh, zs[2], 0, 2, around[0])),
            (3, 9, half(h, yh, zs[0], 1, 15, around[2])),
            (4, 14, half(h, 1 - yh, zs[2], 0, 5, around[0])),
            (6, 12, half(h, 1 - yh, zs[0], 1, 16, around[2])),
        ]

    def ring_forward(h):
        for slot, core_slot, onward in ring_halves(h):
            arrived(h, slot)
            onward.start()
            gather(h, core_slot).start()

    def ring_finish(h):
        for yy, slots_, core_slot in ((yh, (2, 15), 10), (1 - yh, (5, 16), 13)):
            for part in range(2):
                half(h, yy, zs[1], part, slots_[part], sibling).wait_recv()
            gather(h, core_slot).start()

    def sibling_own_row(h):
        for slot in (7, 9, 10, 11):
            arrived(h, slot)

    def sibling_other_row(h):
        for slot in (8, 12, 13, 14):
            arrived(h, slot)

    def stage_a(h, y):
        return remote(send_a.at[h, y], recv_a.at[h, y], rs_send.at[h, y], rs_recv.at[h, y], sibling)

    def stage_c(h):
        return remote(send_c.at[h], recv_c.at[h], rs_send.at[h, 2], rs_recv.at[h, 2], across)

    def stage_b(h, j):
        return remote(send_b.at[h, zs[j]], recv_b.at[h, j], rs_send.at[h, 3 + j], rs_recv.at[h, 3 + j], around[j])

    def stage_x(h, j):
        return remote(send_x.at[h, :, :, xs[j]], recv_x.at[h, j], rs_send.at[h, 6 + j], rs_recv.at[h, 6 + j], beside[j])

    def stage_y(h):
        return remote(send_y.at[h], recv_y.at[h], rs_send.at[h, 9], rs_recv.at[h, 9], over)

    last = heads - 1

    def last_x(j):
        return remote(send_x.at[last, 0, :, xs[j]], recv_x.at[last, j, 0], rs_send.at[last, 6 + j],
                      rs_recv.at[last, 6 + j], beside[j])

    def last_y():
        return remote(send_y.at[last, 0], recv_y.at[last, 0], rs_send.at[last, 9], rs_recv.at[last, 9], over)

    def last_v():
        return remote(send_x.at[last, 1, 1 - yl], recv_v, rs_send.at[last, 10], rs_recv.at[last, 10], over)

    def last_w(j):
        return remote(send_w.at[xs[j]], recv_w.at[j], rs_send.at[last, 11 + j], rs_recv.at[last, 11 + j], beside[j])

    def masks(cc, yy):
        for zz in range(4):
            build_masks((cc * 2 + yy) * 4 + zz, yy * 8 + zz * 2 + cc, src_blocks, table, words, mask_ref)

    for cp in mine_copies[:2]:
        cp.wait()
    pl.semaphore_wait(barrier, 9)
    send_own(0)
    gather(0, 0).start()
    norm_copy.wait()
    for cp in mine_copies[2:]:
        cp.wait()
    for h in range(heads):
        product = qg[h, c, yh, 1, z].astype(F32) * o_all[h].astype(F32)
        nd[c, yh, z, heads + h : heads + h + 1, :] = jnp.sum(product.T, axis=0, keepdims=True)
    send_own(None)
    gather(None, 0).start()
    for h in range(1, heads):
        gather(h, 0).start()
    words_copy.wait()
    table_copy.wait()
    masks(c, yh)
    relay_across(0)
    relay_across(None)
    masks(1 - c, yh)
    masks(c, 1 - yh)
    masks(1 - c, 1 - yh)
    forward_own_row(0)
    forward_own_row(None)

    def exchange_rows(h):
        stage_a(h, 1 - yh).wait_recv()
        send_c[h] = (acc_a[1 - yh] + recv_a[h, 1 - yh].astype(F32)).astype(BF16)
        stage_c(h).start()

    def event_0(h):
        done = h - 1

        @pl.when((h >= 1) & (h < heads))
        def _():
            for j in (0, 2, 1):
                stage_x(done, j).start()

        @pl.when(h == heads)
        def _():
            last_v().start()
            for j in (0, 2, 1):
                last_x(j).start()

        @pl.when(h == 1)
        def _():
            exchange_rows(0)

        @pl.when(h == 0)
        def _():
            send_own(1)
            relay_across(1)

        @pl.when(h == 1)
        def _():
            forward_other_row(1)

        @pl.when((h >= 1) & (h < heads))
        def _():
            sibling_own_row(h)

        @pl.when((h >= 2) & (h <= heads))
        def _():
            for j in range(3):
                stage_x(h - 2, j).wait_recv()
            for a in range(2):
                for y in range(2):
                    keep[lax.rem(h, 2), a, y] = (
                        keep[lax.rem(h, 2), a, y]
                        + recv_x[h - 2, 0, a, y].astype(F32)
                        + recv_x[h - 2, 1, a, y].astype(F32)
                        + recv_x[h - 2, 2, a, y].astype(F32)
                    )
                send_y[h - 2, a] = keep[lax.rem(h, 2), a, 1 - yl].astype(BF16)
            stage_y(h - 2).start()

    def event_1(h):
        @pl.when(h >= 2)
        def _():
            cols = pl.ds(pl.multiple_of((h - 2) * hd, hd), hd)
            for j in range(3):
                stage_b((h - 2), j).wait_recv()
            total = (
                tot_b[z]
                + recv_b[(h - 2), 0].astype(F32)
                + recv_b[(h - 2), 1].astype(F32)
                + recv_b[(h - 2), 2].astype(F32)
            )
            dq_ref[:, cols] = (total * scale).T.astype(BF16)

        @pl.when(h == 0)
        def _():
            sibling_own_row(None)
            sibling_own_row(0)

        @pl.when((h >= 1) & (h < heads))
        def _():
            sibling_other_row(h)

    def event_2(h):
        done = h - 1

        @pl.when((h >= 1) & (h <= heads))
        def _():
            stage_a(done, yh).wait_recv()
            stage_c(done).wait_recv()
            total = acc_a[yh] + recv_a[done, yh].astype(F32) + recv_c[done].astype(F32)
            tot_b[...] = total
            send_b[done] = total.astype(BF16)
            for j in (0, 2, 1):
                stage_b(done, j).start()

        @pl.when(h == heads + 1)
        def _():
            cols = pl.ds(last * hd, hd)
            last_y().wait_recv()
            dk_ref[:, cols] = ((keep[last % 2, 0, yl] + recv_y[last, 0].astype(F32)) * scale).astype(BF16)
            for j in range(3):
                last_w(j).wait_recv()
            dv_ref[:, cols] = (
                tot_w[x] + recv_w[0].astype(F32) + recv_w[1].astype(F32) + recv_w[2].astype(F32)
            ).astype(BF16)

        @pl.when(h == 0)
        def _():
            forward_other_row(None)
            forward_other_row(0)

        @pl.when(h + 1 < heads)
        def _():
            forward_own_row(h + 1)

        @pl.when(h + 2 < heads)
        def _():
            send_own(h + 2)
            relay_across(h + 2)

    def event_3(h):
        done = h - 1

        odd = lax.rem(h + 1, 2)

        @pl.when(h == heads)
        def _():
            last_v().wait_recv()
            total = dv_acc[pl.ds(pl.multiple_of(yl * rows, rows), rows), :].reshape(4, 128, hd) + recv_v[...].astype(F32)
            tot_w[...] = total
            send_w[...] = total.astype(BF16)
            for j in (0, 2, 1):
                last_w(j).start()
            for j in range(3):
                last_x(j).wait_recv()
            for y in range(2):
                keep[odd, 0, y] = (
                    keep[odd, 0, y]
                    + recv_x[last, 0, 0, y].astype(F32)
                    + recv_x[last, 1, 0, y].astype(F32)
                    + recv_x[last, 2, 0, y].astype(F32)
                )
            send_y[last, 0] = keep[odd, 0, 1 - yl].astype(BF16)
            last_y().start()

        @pl.when((h >= 2) & (h <= heads))
        def _():
            cols = pl.ds(pl.multiple_of((h - 2) * hd, hd), hd)
            stage_y(h - 2).wait_recv()
            dk_ref[:, cols] = ((keep[lax.rem(h, 2), 0, yl] + recv_y[h - 2, 0].astype(F32)) * scale).astype(BF16)
            dv_ref[:, cols] = (keep[lax.rem(h, 2), 1, yl] + recv_y[h - 2, 1].astype(F32)).astype(BF16)

        @pl.when(h == 0)
        def _():
            sibling_other_row(None)
            sibling_other_row(0)

        @pl.when((h >= 1) & (h < heads))
        def _():
            exchange_rows(h)

        @pl.when((h >= 1) & (h + 1 < heads))
        def _():
            forward_other_row(h + 1)

    def compute(h, i):
        @pl.when((h == 0) & (i == 0))
        def _():
            for cp in kv_copies:
                cp.wait()

        @pl.when(i == 0)
        def _():
            kt[...] = k_all[h].T
            dk_acc[...] = jnp.zeros_like(dk_acc)
            dv_acc[...] = jnp.zeros_like(dv_acc)

        mine = jnp.where(h == 0, lax.rem(i, 2) == 0, i >= 2)
        own_row = jnp.where(h == 0, i < 2, (i == 0) | (i == 3))
        cc = jnp.where(mine, c, 1 - c)
        yy = jnp.where(own_row, yh, 1 - yh)
        at = pl.multiple_of((cc * 2 + yy) * rows, rows)
        q = qg[h, cc, yy, 0].reshape(rows, hd)
        g = qg[h, cc, yy, 1].reshape(rows, hd)
        norm = jnp.concatenate([nd[cc, yy, j, pl.ds(h, 1), :] for j in range(4)], axis=1) * LOG2E
        delta = jnp.concatenate([nd[cc, yy, j, pl.ds(heads + h, 1), :] for j in range(4)], axis=1)
        dqt = visit(scale, tile, q, g, norm, delta, k_all.at[h], v_all.at[h], kt[...], mask_ref, at,
                    dk_acc, dv_acc, sbuf)

        @pl.when(mine)
        def _():
            for j in range(4):
                acc_a[yy, j] = dqt[:, j * 128 : (j + 1) * 128]

        @pl.when(jnp.logical_not(mine))
        def _():
            for j in range(4):
                send_a[h, yy, j] = dqt[:, j * 128 : (j + 1) * 128].astype(BF16)
            stage_a(h, yy).start()

        @pl.when(i == 3)
        def _():
            for a, acc in enumerate((dk_acc, dv_acc)):
                send_x[h, a] = acc[...].reshape(2, 4, 128, hd).astype(BF16)
                for y in range(2):
                    keep[lax.rem(h, 2), a, y] = acc[pl.ds(pl.multiple_of((y * 4 + x) * 128, 128), 128), :]

    def step(n, carry):
        h = n // 4
        i = lax.rem(n, 4)
        for k, event in enumerate((event_0, event_1, event_2, event_3)):
            @pl.when(i == k)
            def _(event=event):
                event(h)

        @pl.when(h < heads)
        def _():
            compute(h, i)

        return carry

    lax.fori_loop(0, heads * 4 + 7, step, 0)

    def drain_reduce(h):
        for y in range(2):
            stage_a(h, y).wait_send()
        for j in range(3):
            stage_b(h, j).wait_send()
        stage_c(h).wait_send()

    def drain_gather(h, carry):
        for slot in range(15):
            gather(h, slot).wait_send()
        return carry

    def drain(h, carry):
        drain_reduce(h)
        for j in range(3):
            stage_x(h, j).wait_send()
        stage_y(h).wait_send()
        return carry

    for slot in range(15):
        gather(None, slot).wait_send()
        gather(0, slot).wait_send()
    lax.fori_loop(1, heads, drain_gather, 0)
    lax.fori_loop(0, last, drain, 0)
    drain_reduce(last)
    last_v().wait_send()
    last_y().wait_send()
    for j in range(3):
        last_x(j).wait_send()
        last_w(j).wait_send()


def finish(sums_ref, q_out, k_out, v_out):
    for i, out in enumerate((q_out, k_out, v_out)):
        out[...] = sums_ref[i]


def shards(queries, out_grad, outputs, log_norms, src_keys, src_values, block_list, block_count, mask_bits):
    heads = log_norms.shape[0]
    local, features = queries.shape
    hd = features // heads
    n_src = src_keys.shape[0]
    tile = 256
    vmem = pl.BlockSpec(memory_space=pltpu.VMEM)
    anyspace = pl.BlockSpec(memory_space=pl.ANY)
    narrow = jax.ShapeDtypeStruct((local, features), BF16)
    sums = pl.pallas_call(
        functools.partial(core, heads, tile),
        out_shape=jax.ShapeDtypeStruct((3, local, features), BF16),
        in_specs=[pl.BlockSpec(memory_space=pltpu.SMEM), vmem] + [anyspace] * 7,
        out_specs=vmem,
        scratch_shapes=[
            pltpu.VMEM(mask_bits.shape, jnp.int32),
            pltpu.VMEM((8, 128), jnp.int32),
            pltpu.SMEM((8, 128), jnp.int32),
            pltpu.VMEM((n_src, 16 * 128), F32),
            pltpu.VMEM((heads, 2, 2, 2, 4, 128, hd), BF16),
            pltpu.VMEM((heads, 128, hd), BF16),
            pltpu.VMEM((2, 2, 4, 2 * heads, 128), F32),
            pltpu.VMEM((heads, n_src, hd), BF16),
            pltpu.VMEM((heads, n_src, hd), BF16),
            pltpu.VMEM((hd, n_src), BF16),
            pltpu.VMEM((n_src, 512), BF16),
            pltpu.VMEM((n_src, hd), F32),
            pltpu.VMEM((n_src, hd), F32),
            pltpu.VMEM((heads, 2, 4, hd, 128), BF16),
            pltpu.VMEM((heads, 2, 4, hd, 128), BF16),
            pltpu.VMEM((2, 4, hd, 128), F32),
            pltpu.VMEM((heads, 4, hd, 128), BF16),
            pltpu.VMEM((heads, 4, hd, 128), BF16),
            pltpu.VMEM((4, hd, 128), F32),
            pltpu.VMEM((heads, 4, hd, 128), BF16),
            pltpu.VMEM((heads, 3, hd, 128), BF16),
            pltpu.VMEM((heads, 2, 2, 4, 128, hd), BF16),
            pltpu.VMEM((heads, 3, 2, 2, 128, hd), BF16),
            pltpu.VMEM((2, 2, 2, 128, hd), F32),
            pltpu.VMEM((heads, 2, 128, hd), BF16),
            pltpu.VMEM((heads, 2, 128, hd), BF16),
            pltpu.VMEM((4, 128, hd), BF16),
            pltpu.VMEM((4, 128, hd), F32),
            pltpu.VMEM((4, 128, hd), BF16),
            pltpu.VMEM((3, 128, hd), BF16),
            pltpu.SemaphoreType.DMA((heads, 5)),
            pltpu.SemaphoreType.DMA((3,)),
            pltpu.SemaphoreType.DMA((heads, 17)),
            pltpu.SemaphoreType.DMA((heads, 17)),
            pltpu.SemaphoreType.DMA((15,)),
            pltpu.SemaphoreType.DMA((15,)),
            pltpu.SemaphoreType.DMA((heads, 14)),
            pltpu.SemaphoreType.DMA((heads, 14)),
        ],
        compiler_params=pltpu.CompilerParams(
            vmem_limit_bytes=67043328, collective_id=0, has_side_effects=True
        ),
        name="attention",
    )(block_count, block_list, mask_bits, queries, out_grad, outputs, log_norms, src_keys, src_values)
    return pl.pallas_call(
        finish,
        out_shape=(narrow, narrow, narrow),
        in_specs=[vmem],
        out_specs=(vmem, vmem, vmem),
        name="finish",
    )(sums)


def solution(mesh):
    rows = P(("src", "rep"), None)
    placed = (
        rows,
        rows,
        rows,
        P(None, ("src", "rep")),
        P("src", None),
        P("src", None),
        P("src", "rep", None, None),
        P("src", "rep"),
        P("src", "rep", None, None, None),
    )
    return jax.shard_map(shards, mesh=mesh, in_specs=placed, out_specs=(rows, rows, rows), check_vma=False)
```

```python
import functools
import math

import jax
import jax.numpy as jnp
from jax import lax
from jax.experimental import pallas as pl
from jax.experimental.pallas import tpu as pltpu
from jax.sharding import PartitionSpec as P

F32 = jnp.float32
BF16 = jnp.bfloat16
LOG2E = math.log2(math.e)
MESH = pl.DeviceIdType.MESH


def nt_dot(a, b):
    return lax.dot_general(a, b, (((1,), (1,)), ((), ())), preferred_element_type=F32)


def nn_dot(a, b):
    return lax.dot_general(a, b, (((1,), (0,)), ((), ())), preferred_element_type=F32)


def tn_dot(a, b):
    return lax.dot_general(a, b, (((0,), (0,)), ((), ())), preferred_element_type=F32)


def build_masks(u, dest, src_blocks, table, words_ref, mask_ref):
    row = lax.broadcasted_iota(jnp.int32, (16, 128), 0)
    lane = lax.broadcasted_iota(jnp.int32, (16, 128), 1)
    half = jnp.where(lax.rem(lane, 16) >= 8, 8, 0)
    spread = jnp.where(row == lane // 16 + half, 1.0, 0.0).astype(BF16)
    bit = jnp.left_shift(1, lax.rem(lax.broadcasted_iota(jnp.int32, (1, 128), 1), 8))
    words = jnp.concatenate(
        [
            words_ref[0, 0, jnp.clip(table[0, dest * src_blocks + j], 0, words_ref.shape[2] - 1)] * table[1, dest * src_blocks + j]
            for j in range(src_blocks)
        ],
        axis=1,
    )
    halves = jnp.concatenate(
        [jnp.bitwise_and(words, 255), jnp.bitwise_and(jnp.right_shift(words, 8), 255)], axis=0
    )
    wide = tn_dot(halves.astype(F32).astype(BF16), spread).astype(jnp.int32)
    picked = jnp.where(jnp.bitwise_and(wide, bit) != 0, 0.0, -1e30)
    mask_ref[:, pl.ds(pl.multiple_of(u * 128, 128), 128)] = picked


def visit(scale, tile, q, g, norm, delta, k_ref, v_ref, kt, mask_ref, at, dk_ref, dv_ref, sbuf):
    n_src = k_ref.shape[0]
    rows = q.shape[0]
    for c in range(n_src // tile):
        cs = pl.ds(c * tile, tile)
        s = nt_dot(k_ref[cs, :], q)
        p = jnp.exp2((s * (scale * LOG2E) - norm) + mask_ref[cs, pl.ds(at, rows)])
        d = nt_dot(v_ref[cs, :], g)
        ds = p * (d - delta)
        p_low = p.astype(BF16)
        s_low = ds.astype(BF16)
        sbuf[cs, :] = s_low
        dv_ref[cs, :] += nn_dot(p_low, g)
        dk_ref[cs, :] += nn_dot(s_low, q)
    return nn_dot(kt, sbuf[...])


def pair_slots(list_ref, count, src_blocks, n_pairs):
    capacity = list_ref.shape[3]
    code = list_ref[0, 0, 0:1, :] * src_blocks + list_ref[0, 0, 1:2, :]
    order = lax.broadcasted_iota(jnp.int32, (n_pairs, capacity), 1)
    pair = lax.broadcasted_iota(jnp.int32, (n_pairs, capacity), 0)
    hit = (code == pair) & (order < count)
    slot = jnp.sum(jnp.where(hit, order, 0), axis=1, keepdims=True)
    live = jnp.sum(jnp.where(hit, 1, 0), axis=1, keepdims=True)
    column = lax.broadcasted_iota(jnp.int32, (n_pairs, 128), 1)
    both = jnp.where(column == 0, slot, jnp.where(column == 1, live, 0))
    return both.T[0:8]


def core(heads, tile, count_ref, list_ref, words_hbm, q_hbm, g_hbm, o_hbm, norm_hbm, k_hbm, v_hbm,
         out_ref,
         words, slots, table, mask_ref, qg, o_all, nd, k_all, v_all, kt, sbuf, dk_acc, dv_acc,
         send_a, recv_a, acc_a, send_c, recv_c, tot_b, send_b, recv_b,
         send_x, recv_x, keep, send_y, recv_y, recv_v, tot_w, send_w, recv_w,
         local_sem, extra_sem, ag_send, ag_recv, nd_send, nd_recv, rs_send, rs_recv):
    dq_ref, dk_ref, dv_ref = out_ref.at[0], out_ref.at[1], out_ref.at[2]
    hd = kt.shape[0]
    n_src = kt.shape[1]
    src_blocks = n_src // 128
    rows = 4 * 128
    scale = hd ** -0.5
    src, rep = lax.axis_index("src"), lax.axis_index("rep")
    yh, z, c = src // 8, lax.rem(src, 8) // 2, lax.rem(src, 2)
    yl, x = rep // 4, lax.rem(rep, 4)

    def at_src(yy, zz, cc):
        return {"src": yy * 8 + zz * 2 + cc, "rep": rep}

    def at_rep(yy, xx):
        return {"src": src, "rep": yy * 4 + xx}

    sibling = at_src(yh, z, 1 - c)
    across = at_src(1 - yh, z, c)
    zs = [lax.rem(z + d, 4) for d in (1, 2, 3)]
    xs = [lax.rem(x + d, 4) for d in (1, 2, 3)]
    around = [at_src(yh, zz, c) for zz in zs]
    beside = [at_rep(yl, xx) for xx in xs]
    over = at_rep(1 - yl, x)

    barrier = pltpu.get_barrier_semaphore()
    for peer in [sibling, across, over] + around + beside:
        pl.semaphore_signal(barrier, inc=1, device_id=peer, device_id_type=MESH)

    mine_copies, kv_copies = [], []
    for h in range(heads):
        cols = pl.ds(h * hd, hd)
        for i, (a, b) in enumerate((
            (q_hbm, qg.at[h, c, yh, 0, z]), (g_hbm, qg.at[h, c, yh, 1, z]), (o_hbm, o_all.at[h]),
            (k_hbm, k_all.at[h]), (v_hbm, v_all.at[h]),
        )):
            cp = pltpu.make_async_copy(a.at[:, cols], b, local_sem.at[h, i])
            if i < 3:
                cp.start()
                mine_copies.append(cp)
            else:
                kv_copies.append(cp)
    norm_copy = pltpu.make_async_copy(norm_hbm, nd.at[c, yh, z, pl.ds(0, heads)], extra_sem.at[0])
    norm_copy.start()
    words_copy = pltpu.make_async_copy(words_hbm, words, extra_sem.at[1])
    words_copy.start()
    for cp in kv_copies:
        cp.start()

    slots[...] = pair_slots(list_ref, count_ref[0, 0], src_blocks, 128)
    table_copy = pltpu.make_async_copy(slots, table, extra_sem.at[2])
    table_copy.start()

    def remote(a, b, s, r, peer):
        return pltpu.make_async_remote_copy(
            src_ref=a, dst_ref=b, send_sem=s, recv_sem=r, device_id=peer, device_id_type=MESH
        )

    def gather_copy(h, cc, yy, zz, slot, peer):
        if h is None:
            ref = nd.at[cc, yy, zz]
            return remote(ref, ref, nd_send.at[slot], nd_recv.at[slot], peer)
        ref = qg.at[h, cc, yy, :, zz]
        return remote(ref, ref, ag_send.at[h, slot], ag_recv.at[h, slot], peer)

    def gather(h, slot):
        if slot == 0:
            yy, zz, peer = yh, z, across
        elif slot < 4:
            yy, zz, peer = yh, z, around[slot - 1]
        elif slot < 7:
            yy, zz, peer = 1 - yh, z, around[slot - 4]
        elif slot == 7:
            yy, zz, peer = yh, z, sibling
        elif slot == 8:
            yy, zz, peer = 1 - yh, z, sibling
        elif slot < 12:
            yy, zz, peer = yh, zs[slot - 9], sibling
        else:
            yy, zz, peer = 1 - yh, zs[slot - 12], sibling
        return gather_copy(h, c, yy, zz, slot, peer)

    def arrived(h, slot):
        if slot == 0:
            cc, yy, zz = c, 1 - yh, z
        elif slot < 4:
            cc, yy, zz = c, yh, zs[3 - slot]
        elif slot < 7:
            cc, yy, zz = c, 1 - yh, zs[6 - slot]
        elif slot == 7:
            cc, yy, zz = 1 - c, yh, z
        elif slot == 8:
            cc, yy, zz = 1 - c, 1 - yh, z
        elif slot < 12:
            cc, yy, zz = 1 - c, yh, zs[slot - 9]
        else:
            cc, yy, zz = 1 - c, 1 - yh, zs[slot - 12]
        gather_copy(h, cc, yy, zz, slot, sibling).wait_recv()

    def send_own(h):
        for slot in (2, 1, 3, 7):
            gather(h, slot).start()

    def relay_across(h):
        arrived(h, 0)
        for slot in (5, 4, 6, 8):
            gather(h, slot).start()

    def forward_own_row(h):
        for d in (1, 3, 2):
            arrived(h, d)
            gather(h, 12 - d).start()

    def forward_other_row(h):
        for d in (1, 3, 2):
            arrived(h, 3 + d)
            gather(h, 15 - d).start()

    def half(h, yy, zz, part, slot, peer):
        ref = qg.at[h, c, yy, part, zz]
        return remote(ref, ref, ag_send.at[h, slot], ag_recv.at[h, slot], peer)

    def ring_own(h):
        for slot in (1, 3, 7):
            gather(h, slot).start()

    def ring_across(h):
        arrived(h, 0)
        for slot in (4, 6, 8):
            gather(h, slot).start()

    def ring_halves(h):
        return [
            (1, 11, half(h, yh, zs[2], 0, 2, around[0])),
            (3, 9, half(h, yh, zs[0], 1, 15, around[2])),
            (4, 14, half(h, 1 - yh, zs[2], 0, 5, around[0])),
            (6, 12, half(h, 1 - yh, zs[0], 1, 16, around[2])),
        ]

    def ring_forward(h):
        for slot, core_slot, onward in ring_halves(h):
            arrived(h, slot)
            onward.start()
            gather(h, core_slot).start()

    def ring_finish(h):
        for yy, slots_, core_slot in ((yh, (2, 15), 10), (1 - yh, (5, 16), 13)):
            for part in range(2):
                half(h, yy, zs[1], part, slots_[part], sibling).wait_recv()
            gather(h, core_slot).start()

    def sibling_own_row(h):
        for slot in (7, 9, 10, 11):
            arrived(h, slot)

    def sibling_other_row(h):
        for slot in (8, 12, 13, 14):
            arrived(h, slot)

    def stage_a(h, y):
        return remote(send_a.at[h, y], recv_a.at[h, y], rs_send.at[h, y], rs_recv.at[h, y], sibling)

    def stage_c(h):
        return remote(send_c.at[h], recv_c.at[h], rs_send.at[h, 2], rs_recv.at[h, 2], across)

    def stage_b(h, j):
        return remote(send_b.at[h, zs[j]], recv_b.at[h, j], rs_send.at[h, 3 + j], rs_recv.at[h, 3 + j], around[j])

    def stage_x(h, j):
        return remote(send_x.at[h, :, :, xs[j]], recv_x.at[h, j], rs_send.at[h, 6 + j], rs_recv.at[h, 6 + j], beside[j])

    def stage_y(h):
        return remote(send_y.at[h], recv_y.at[h], rs_send.at[h, 9], rs_recv.at[h, 9], over)

    last = heads - 1

    def last_x(j):
        return remote(send_x.at[last, 0, :, xs[j]], recv_x.at[last, j, 0], rs_send.at[last, 6 + j],
                      rs_recv.at[last, 6 + j], beside[j])

    def last_y():
        return remote(send_y.at[last, 0], recv_y.at[last, 0], rs_send.at[last, 9], rs_recv.at[last, 9], over)

    def last_v():
        return remote(send_x.at[last, 1, 1 - yl], recv_v, rs_send.at[last, 10], rs_recv.at[last, 10], over)

    def last_w(j):
        return remote(send_w.at[xs[j]], recv_w.at[j], rs_send.at[last, 11 + j], rs_recv.at[last, 11 + j], beside[j])

    def masks(cc, yy):
        for zz in range(4):
            build_masks((cc * 2 + yy) * 4 + zz, yy * 8 + zz * 2 + cc, src_blocks, table, words, mask_ref)

    for cp in mine_copies[:2]:
        cp.wait()
    pl.semaphore_wait(barrier, 9)
    send_own(0)
    gather(0, 0).start()
    norm_copy.wait()
    for cp in mine_copies[2:]:
        cp.wait()
    for h in range(heads):
        product = qg[h, c, yh, 1, z].astype(F32) * o_all[h].astype(F32)
        nd[c, yh, z, heads + h : heads + h + 1, :] = jnp.sum(product.T, axis=0, keepdims=True)
    send_own(None)
    gather(None, 0).start()
    for h in range(1, heads):
        gather(h, 0).start()
    words_copy.wait()
    table_copy.wait()
    masks(c, yh)
    relay_across(0)
    relay_across(None)
    masks(1 - c, yh)
    masks(c, 1 - yh)
    masks(1 - c, 1 - yh)
    forward_own_row(0)
    forward_own_row(None)

    def exchange_rows(h):
        stage_a(h, 1 - yh).wait_recv()
        send_c[h] = (acc_a[1 - yh] + recv_a[h, 1 - yh].astype(F32)).astype(BF16)
        stage_c(h).start()

    def event_0(h):
        done = h - 1

        @pl.when((h >= 1) & (h < heads))
        def _():
            for j in (1, 0, 2):
                stage_x(done, j).start()

        @pl.when(h == heads)
        def _():
            last_v().start()
            for j in (1, 0, 2):
                last_x(j).start()

        @pl.when(h == 1)
        def _():
            exchange_rows(0)

        @pl.when(h == 0)
        def _():
            send_own(1)
            relay_across(1)

        @pl.when(h == 1)
        def _():
            forward_other_row(1)

        @pl.when((h >= 1) & (h < heads))
        def _():
            sibling_own_row(h)

        @pl.when((h >= 2) & (h <= heads))
        def _():
            for j in range(3):
                stage_x(h - 2, j).wait_recv()
            for a in range(2):
                for y in range(2):
                    keep[lax.rem(h, 2), a, y] = (
                        keep[lax.rem(h, 2), a, y]
                        + recv_x[h - 2, 0, a, y].astype(F32)
                        + recv_x[h - 2, 1, a, y].astype(F32)
                        + recv_x[h - 2, 2, a, y].astype(F32)
                    )
                send_y[h - 2, a] = keep[lax.rem(h, 2), a, 1 - yl].astype(BF16)
            stage_y(h - 2).start()

    def event_1(h):
        @pl.when(h >= 2)
        def _():
            cols = pl.ds(pl.multiple_of((h - 2) * hd, hd), hd)
            for j in range(3):
                stage_b((h - 2), j).wait_recv()
            total = (
                tot_b[z]
                + recv_b[(h - 2), 0].astype(F32)
                + recv_b[(h - 2), 1].astype(F32)
                + recv_b[(h - 2), 2].astype(F32)
            )
            dq_ref[:, cols] = (total * scale).T.astype(BF16)

        @pl.when(h == 0)
        def _():
            sibling_own_row(None)
            sibling_own_row(0)

        @pl.when((h >= 1) & (h < heads))
        def _():
            sibling_other_row(h)

    def event_2(h):
        done = h - 1

        @pl.when((h >= 1) & (h <= heads))
        def _():
            stage_a(done, yh).wait_recv()
            stage_c(done).wait_recv()
            total = acc_a[yh] + recv_a[done, yh].astype(F32) + recv_c[done].astype(F32)
            tot_b[...] = total
            send_b[done] = total.astype(BF16)
            for j in (1, 0, 2):
                stage_b(done, j).start()

        @pl.when(h == heads + 1)
        def _():
            cols = pl.ds(last * hd, hd)
            last_y().wait_recv()
            dk_ref[:, cols] = ((keep[last % 2, 0, yl] + recv_y[last, 0].astype(F32)) * scale).astype(BF16)
            for j in range(3):
                last_w(j).wait_recv()
            dv_ref[:, cols] = (
                tot_w[x] + recv_w[0].astype(F32) + recv_w[1].astype(F32) + recv_w[2].astype(F32)
            ).astype(BF16)

        @pl.when(h == 0)
        def _():
            forward_other_row(None)
            forward_other_row(0)

        @pl.when(h + 1 < heads)
        def _():
            forward_own_row(h + 1)

        @pl.when(h + 2 < heads)
        def _():
            send_own(h + 2)
            relay_across(h + 2)

    def event_3(h):
        done = h - 1

        odd = lax.rem(h + 1, 2)

        @pl.when(h == heads)
        def _():
            last_v().wait_recv()
            total = dv_acc[pl.ds(pl.multiple_of(yl * rows, rows), rows), :].reshape(4, 128, hd) + recv_v[...].astype(F32)
            tot_w[...] = total
            send_w[...] = total.astype(BF16)
            for j in (1, 0, 2):
                last_w(j).start()
            for j in range(3):
                last_x(j).wait_recv()
            for y in range(2):
                keep[odd, 0, y] = (
                    keep[odd, 0, y]
                    + recv_x[last, 0, 0, y].astype(F32)
                    + recv_x[last, 1, 0, y].astype(F32)
                    + recv_x[last, 2, 0, y].astype(F32)
                )
            send_y[last, 0] = keep[odd, 0, 1 - yl].astype(BF16)
            last_y().start()

        @pl.when((h >= 2) & (h <= heads))
        def _():
            cols = pl.ds(pl.multiple_of((h - 2) * hd, hd), hd)
            stage_y(h - 2).wait_recv()
            dk_ref[:, cols] = ((keep[lax.rem(h, 2), 0, yl] + recv_y[h - 2, 0].astype(F32)) * scale).astype(BF16)
            dv_ref[:, cols] = (keep[lax.rem(h, 2), 1, yl] + recv_y[h - 2, 1].astype(F32)).astype(BF16)

        @pl.when(h == 0)
        def _():
            sibling_other_row(None)
            sibling_other_row(0)

        @pl.when((h >= 1) & (h < heads))
        def _():
            exchange_rows(h)

        @pl.when((h >= 1) & (h + 1 < heads))
        def _():
            forward_other_row(h + 1)

    def compute(h, i):
        @pl.when((h == 0) & (i == 0))
        def _():
            for cp in kv_copies:
                cp.wait()

        @pl.when(i == 0)
        def _():
            kt[...] = k_all[h].T
            dk_acc[...] = jnp.zeros_like(dk_acc)
            dv_acc[...] = jnp.zeros_like(dv_acc)

        mine = jnp.where(h == 0, lax.rem(i, 2) == 0, i >= 2)
        own_row = jnp.where(h == 0, i < 2, (i == 0) | (i == 3))
        cc = jnp.where(mine, c, 1 - c)
        yy = jnp.where(own_row, yh, 1 - yh)
        at = pl.multiple_of((cc * 2 + yy) * rows, rows)
        q = qg[h, cc, yy, 0].reshape(rows, hd)
        g = qg[h, cc, yy, 1].reshape(rows, hd)
        norm = jnp.concatenate([nd[cc, yy, j, pl.ds(h, 1), :] for j in range(4)], axis=1) * LOG2E
        delta = jnp.concatenate([nd[cc, yy, j, pl.ds(heads + h, 1), :] for j in range(4)], axis=1)
        dqt = visit(scale, tile, q, g, norm, delta, k_all.at[h], v_all.at[h], kt[...], mask_ref, at,
                    dk_acc, dv_acc, sbuf)

        @pl.when(mine)
        def _():
            for j in range(4):
                acc_a[yy, j] = dqt[:, j * 128 : (j + 1) * 128]

        @pl.when(jnp.logical_not(mine))
        def _():
            for j in range(4):
                send_a[h, yy, j] = dqt[:, j * 128 : (j + 1) * 128].astype(BF16)
            stage_a(h, yy).start()

        @pl.when(i == 3)
        def _():
            for a, acc in enumerate((dk_acc, dv_acc)):
                send_x[h, a] = acc[...].reshape(2, 4, 128, hd).astype(BF16)
                for y in range(2):
                    keep[lax.rem(h, 2), a, y] = acc[pl.ds(pl.multiple_of((y * 4 + x) * 128, 128), 128), :]

    def step(n, carry):
        h = n // 4
        i = lax.rem(n, 4)
        for k, event in enumerate((event_0, event_1, event_2, event_3)):
            @pl.when(i == k)
            def _(event=event):
                event(h)

        @pl.when(h < heads)
        def _():
            compute(h, i)

        return carry

    lax.fori_loop(0, heads * 4 + 7, step, 0)

    def drain_reduce(h):
        for y in range(2):
            stage_a(h, y).wait_send()
        for j in range(3):
            stage_b(h, j).wait_send()
        stage_c(h).wait_send()

    def drain_gather(h, carry):
        for slot in range(15):
            gather(h, slot).wait_send()
        return carry

    def drain(h, carry):
        drain_reduce(h)
        for j in range(3):
            stage_x(h, j).wait_send()
        stage_y(h).wait_send()
        return carry

    for slot in range(15):
        gather(None, slot).wait_send()
        gather(0, slot).wait_send()
    lax.fori_loop(1, heads, drain_gather, 0)
    lax.fori_loop(0, last, drain, 0)
    drain_reduce(last)
    last_v().wait_send()
    last_y().wait_send()
    for j in range(3):
        last_x(j).wait_send()
        last_w(j).wait_send()


def finish(sums_ref, q_out, k_out, v_out):
    for i, out in enumerate((q_out, k_out, v_out)):
        out[...] = sums_ref[i]


def shards(queries, out_grad, outputs, log_norms, src_keys, src_values, block_list, block_count, mask_bits):
    heads = log_norms.shape[0]
    local, features = queries.shape
    hd = features // heads
    n_src = src_keys.shape[0]
    tile = 256
    vmem = pl.BlockSpec(memory_space=pltpu.VMEM)
    anyspace = pl.BlockSpec(memory_space=pl.ANY)
    narrow = jax.ShapeDtypeStruct((local, features), BF16)
    sums = pl.pallas_call(
        functools.partial(core, heads, tile),
        out_shape=jax.ShapeDtypeStruct((3, local, features), BF16),
        in_specs=[pl.BlockSpec(memory_space=pltpu.SMEM), vmem] + [anyspace] * 7,
        out_specs=vmem,
        scratch_shapes=[
            pltpu.VMEM(mask_bits.shape, jnp.int32),
            pltpu.VMEM((8, 128), jnp.int32),
            pltpu.SMEM((8, 128), jnp.int32),
            pltpu.VMEM((n_src, 16 * 128), F32),
            pltpu.VMEM((heads, 2, 2, 2, 4, 128, hd), BF16),
            pltpu.VMEM((heads, 128, hd), BF16),
            pltpu.VMEM((2, 2, 4, 2 * heads, 128), F32),
            pltpu.VMEM((heads, n_src, hd), BF16),
            pltpu.VMEM((heads, n_src, hd), BF16),
            pltpu.VMEM((hd, n_src), BF16),
            pltpu.VMEM((n_src, 512), BF16),
            pltpu.VMEM((n_src, hd), F32),
            pltpu.VMEM((n_src, hd), F32),
            pltpu.VMEM((heads, 2, 4, hd, 128), BF16),
            pltpu.VMEM((heads, 2, 4, hd, 128), BF16),
            pltpu.VMEM((2, 4, hd, 128), F32),
            pltpu.VMEM((heads, 4, hd, 128), BF16),
            pltpu.VMEM((heads, 4, hd, 128), BF16),
            pltpu.VMEM((4, hd, 128), F32),
            pltpu.VMEM((heads, 4, hd, 128), BF16),
            pltpu.VMEM((heads, 3, hd, 128), BF16),
            pltpu.VMEM((heads, 2, 2, 4, 128, hd), BF16),
            pltpu.VMEM((heads, 3, 2, 2, 128, hd), BF16),
            pltpu.VMEM((2, 2, 2, 128, hd), F32),
            pltpu.VMEM((heads, 2, 128, hd), BF16),
            pltpu.VMEM((heads, 2, 128, hd), BF16),
            pltpu.VMEM((4, 128, hd), BF16),
            pltpu.VMEM((4, 128, hd), F32),
            pltpu.VMEM((4, 128, hd), BF16),
            pltpu.VMEM((3, 128, hd), BF16),
            pltpu.SemaphoreType.DMA((heads, 5)),
            pltpu.SemaphoreType.DMA((3,)),
            pltpu.SemaphoreType.DMA((heads, 17)),
            pltpu.SemaphoreType.DMA((heads, 17)),
            pltpu.SemaphoreType.DMA((15,)),
            pltpu.SemaphoreType.DMA((15,)),
            pltpu.SemaphoreType.DMA((heads, 14)),
            pltpu.SemaphoreType.DMA((heads, 14)),
        ],
        compiler_params=pltpu.CompilerParams(
            vmem_limit_bytes=67043328, collective_id=0, has_side_effects=True
        ),
        name="attention",
    )(block_count, block_list, mask_bits, queries, out_grad, outputs, log_norms, src_keys, src_values)
    return pl.pallas_call(
        finish,
        out_shape=(narrow, narrow, narrow),
        in_specs=[vmem],
        out_specs=(vmem, vmem, vmem),
        name="finish",
    )(sums)


def solution(mesh):
    rows = P(("src", "rep"), None)
    placed = (
        rows,
        rows,
        rows,
        P(None, ("src", "rep")),
        P("src", None),
        P("src", None),
        P("src", "rep", None, None),
        P("src", "rep"),
        P("src", "rep", None, None, None),
    )
    return jax.shard_map(shards, mesh=mesh, in_specs=placed, out_specs=(rows, rows, rows), check_vma=False)
```
